256 devices in a mesh: rve: 8 (over x, y_hi), slab: 32 (over y_lo, z, core).
Axes of the slice: x: 4, y: 4 (y_hi: 2, y_lo: 2; y = y_hi * 2 + y_lo), z: 8, core: 2. Of those that a mesh axis runs over, the one named last changes fastest.
Arguments:
- displacement: float32 [128, 3, 256, 256], P('slab', None, 'rve'), parts along dimension 2, may hold values from -6 to 6
- load: float32 [128, 3, 256, 256], P('slab', None, 'rve'), parts along dimension 2, may hold values from -24 to 24
- phase: int32 [128, 256, 256], P('slab', 'rve'), parts along dimension 1, may hold values from 0 to 2
- moduli: float32 [2, 3], replicated, may hold values from 0.5 to 4
Outputs:
- solution: float32 [128, 3, 256, 256], P('slab', None, 'rve'), parts along dimension 2
- residual: float32 [128, 3, 256, 256], P('slab', None, 'rve'), parts along dimension 2
The draws below stay inside these ranges and needn't reach their ends.
There are 8 independent parts, one for each index of `rve`. The reference program is written for one: setup_inputs(seed, part) draws one part's arguments, and reference() takes and returns one part's arrays. A program takes and returns all parts, laid end to end along the dimension named above; an argument that names none is the same for every part. Nothing has to cross between parts.
All inputs are finite; a program needn't handle non-finite values.
Results may differ from the reference program's by a relative error of at most 0.00002.
Values sent between devices are 32-bit elements; how exact they have to be, the bound alone decides.
No kernel may reach another device: no remote copies, remote signals or barrier semaphores. Data moves between devices by JAX's collectives and lax.ppermute only.
A program may use at most 64 MiB of HBM per device.

```python
import math
import jax
import jax.numpy as jnp

NX = 32
NY = 256
PHASES = 3
SWEEPS = 6
NZ = 128


def place_ends(result, key, least, largest):
    dims = result.shape
    index_at = [jax.random.randint(jax.random.fold_in(key, axis), (), 0, dims[axis]) for axis in range(len(dims))]
    result = result.at[tuple(index_at)].set(least)
    longest = dims.index(max(dims))
    index_at[longest] = (index_at[longest] + 1) % dims[longest]
    return result.at[tuple(index_at)].set(largest)


def level_of(key, extent, shards, least, largest):
    loudness, own = 1.0, jax.random.fold_in(key, 6)
    for axis_at, shards_of in shards:
        heights = jnp.exp(jax.random.uniform(jax.random.fold_in(own, axis_at), (shards_of,), jnp.float32, least / len(shards), largest / len(shards)))
        loudness = loudness * jnp.repeat(heights, extent[axis_at] // shards_of).reshape([-1 if axis == axis_at else 1 for axis in range(len(extent))])
    return loudness


def gaussian(own_key, shape, scale, reach, cuts=(), kind=jnp.bfloat16):
    result = scale * jax.random.normal(own_key, shape, jnp.float32)
    if cuts:
        result = result * level_of(own_key, shape, cuts, -0.22, 0.18)
    return jnp.clip(result, -reach, reach).astype(kind)


def setup_inputs(seed: int = 0, part: int = 0) -> dict:
    streams_of = jax.random.split(jax.random.key(seed), 5)
    part_keys = jax.random.split(jax.random.fold_in(streams_of[4], part), 5)
    return {
        "displacement": gaussian(part_keys[0], (NZ, 3, NX, NY), 1.0, 6.0, ((0, 32),), jnp.float32),
        "load": gaussian(part_keys[1], (NZ, 3, NX, NY), 4.0, 24.0, ((0, 32),), jnp.float32),
        "phase": place_ends(jax.random.randint(part_keys[2], (NZ, NX, NY), 0, PHASES), jax.random.fold_in(part_keys[2], 1), 0, PHASES - 1).astype(jnp.int32),
        "moduli": jnp.clip(jnp.exp(jax.random.uniform(streams_of[3], (2, PHASES), jnp.float32, math.log(0.5), math.log(4.0))), 0.5, 4.0),
    }


def plus_next(value, axis):
    return value + jnp.roll(value, -1, axis)


def minus_next(value, axis):
    return jnp.roll(value, -1, axis) - value


def plus_prev(value, axis):
    return value + jnp.roll(value, 1, axis)


def prev_minus(value, axis):
    return jnp.roll(value, 1, axis) - value


def materials(phase, moduli):
    lame = jnp.zeros(phase.shape, jnp.float32)
    shear = jnp.zeros(phase.shape, jnp.float32)
    for index in range(moduli.shape[1]):
        select = (phase == index).astype(jnp.float32)
        lame = lame + select * moduli[0, index]
        shear = shear + select * moduli[1, index]
    return lame, shear


def element_terms(lower, upper, lame, shear):
    total = lower + upper
    jump = upper - lower
    grad_x = 0.25 * minus_next(plus_next(total, -1), -2)
    grad_y = 0.25 * plus_next(minus_next(total, -1), -2)
    grad_z = 0.25 * plus_next(plus_next(jump, -1), -2)
    trace = grad_x[:, 0] + grad_y[:, 1] + grad_z[:, 2]
    normal_x = lame * trace + 2.0 * shear * grad_x[:, 0]
    normal_y = lame * trace + 2.0 * shear * grad_y[:, 1]
    normal_z = lame * trace + 2.0 * shear * grad_z[:, 2]
    shear_xy = shear * (grad_y[:, 0] + grad_x[:, 1])
    shear_xz = shear * (grad_z[:, 0] + grad_x[:, 2])
    shear_yz = shear * (grad_z[:, 1] + grad_y[:, 2])
    col_x = jnp.stack([normal_x, shear_xy, shear_xz], 1)
    col_y = jnp.stack([shear_xy, normal_y, shear_yz], 1)
    col_z = jnp.stack([shear_xz, shear_yz, normal_z], 1)
    inplane = 0.25 * (plus_prev(prev_minus(col_x, -2), -1) + plus_prev(prev_minus(col_y, -1), -2))
    vertical = 0.25 * plus_prev(plus_prev(col_z, -1), -2)
    return inplane, vertical


def operate(field, lame, shear):
    inplane, vertical = element_terms(field, jnp.roll(field, -1, 0), lame, shear)
    return inplane + jnp.roll(inplane, 1, 0) + jnp.roll(vertical, 1, 0) - vertical


def reference(displacement, load, phase, moduli):
    lame, shear = materials(phase, moduli)
    stiff = lame + 4.0 * shear
    diagonal = plus_prev(plus_prev(plus_prev(stiff, -1), -2), 0) / 16.0
    diagonal = diagonal[:, None]
    field = displacement
    for sweep in range(SWEEPS):
        field = field + 0.5 * (load - operate(field, lame, shear)) / diagonal
    return field, load - operate(field, lame, shear)
```

```python
import jax
import jax.numpy as jnp
from jax import lax
from jax.experimental import pallas as pl
from jax.experimental.pallas import tpu as pltpu
from jax.sharding import PartitionSpec as P


OWN = 4
DEPTH = 6
INNER = 3
NODES = DEPTH + OWN + INNER
LAYERS = 16
N0 = DEPTH
L0 = 8

VMEM = pl.BlockSpec(memory_space=pltpu.VMEM)
SMEM = pl.BlockSpec(memory_space=pltpu.SMEM)
HBM = pl.BlockSpec(memory_space=pltpu.HBM)
ROW = (4, 8, 256)


def f32(*shape):
    return jax.ShapeDtypeStruct(shape + ROW, jnp.float32)


def even_rows():
    return lax.broadcasted_iota(jnp.int32, (8, 128), 0) % 2 == 0


def load_raw(ref, index, r):
    a = ref[index + (pl.ds(r, 8, stride=8), slice(None))]
    b = ref[index + (pl.ds(r + 4, 8, stride=8), slice(None))]
    even = even_rows()
    low = jnp.where(even, a, pltpu.roll(b, 1, 0))
    high = jnp.where(even, pltpu.roll(a, 7, 0), b)
    return jnp.concatenate([low, high], axis=1)


def store_raw(ref, index, r, value):
    low, high = value[:, :128], value[:, 128:]
    even = even_rows()
    ref[index + (pl.ds(r, 8, stride=8), slice(None))] = jnp.where(even, low, pltpu.roll(high, 1, 0))
    ref[index + (pl.ds(r + 4, 8, stride=8), slice(None))] = jnp.where(even, pltpu.roll(low, 7, 0), high)


def y_next(v):
    return pltpu.roll(v, 255, 1)


def y_prev(v):
    return pltpu.roll(v, 1, 1)


def x_prev(rows, r):
    return rows[r - 1] if r > 0 else pltpu.roll(rows[3], 1, 0)


def y_stage(sm, get, m):
    for c in range(3):
        for r in range(4):
            d = get(m, c, r)
            n = y_next(d)
            sm[m + L0, c, r] = d + n
            sm[m + L0, 3 + c, r] = n - d


def stress_step(sm, st, lm, m, get):
    first = prev = None

    def stress(z, nxt, r):
        x0, y1, z2, _, _, e, pd, qd = z
        gxx = nxt[0] - x0
        gyy = nxt[1] + y1
        gzz = nxt[2] + z2
        lame, mu = lm[m + L0, 0, r], lm[m + L0, 1, r]
        lt = lame * (gxx + gyy + gzz)
        mu2 = mu + mu
        st[m + L0, 0, r] = lt + mu2 * gxx
        st[m + L0, 1, r] = mu * (nxt[3] + pd)
        st[m + L0, 2, r] = lt + mu2 * gyy
        st[m + L0, 3, r] = mu * (nxt[4] + qd)
        st[m + L0, 4, r] = mu * (nxt[5] + e)
        st[m + L0, 5, r] = lt + mu2 * gzz

    for r in range(4):
        s, my, j = [], [], []
        for c in range(3):
            d = get(m + 1, c, r)
            n = y_next(d)
            su, mu_ = d + n, n - d
            sl, ml = sm[m + L0, c, r], sm[m + L0, 3 + c, r]
            sm[m + 1 + L0, c, r] = su
            sm[m + 1 + L0, 3 + c, r] = mu_
            s.append(sl + su)
            my.append(ml + mu_)
            j.append(su - sl)
        z = (s[0], my[1], j[2], my[0] + s[1], j[0] + s[2], j[1] + my[2], my[0] - s[1], j[0] - s[2])
        if r == 0:
            first = z
        else:
            stress(prev, z, r - 1)
        prev = z
    stress(prev, tuple(pltpu.roll(v, 7, 0) for v in first[:6]), 3)


def node_sums(st, m, r, above, below):
    new = [st[m + L0, i, r] if above else None for i in range(6)]
    old = [st[m - 1 + L0, i, r] if below else None for i in range(6)]

    def plus(i):
        return new[i] if not below else old[i] if not above else new[i] + old[i]

    def minus(i):
        return -new[i] if not below else old[i] if not above else old[i] - new[i]

    xx, xy, yy, xz, yz = (plus(i) for i in range(5))
    dxz, dyz, dzz = (minus(i) for i in range(3, 6))
    return (
        (xx + dxz, xy + dyz, xz + dzz),
        (dxz - xx, dyz - xy, dzz - xz),
        (xy, yy, yz),
    )


def node_step(st, m, finish, above=True, below=True):
    first = prev = None

    def out(pq, pp, ph, r):
        for c in range(3):
            g = pp[c] + pq[1][c]
            hh = ph[c] + pq[2][c]
            finish(m, c, r, (g - hh) + y_prev(g + hh))

    for r in range(4):
        pq = node_sums(st, m, r, above, below)
        if r == 0:
            first = pq
        else:
            out(pq, prev[0], prev[2], r)
        prev = pq
    roll = lambda v: pltpu.roll(v, 1, 0)
    out(first, tuple(map(roll, prev[0])), tuple(map(roll, prev[2])), 0)


def advance(refs, s, lo, hi):
    R, W, LM, U, sm, st = refs
    src, dst = s % 2, (s + 1) % 2

    def get(m, c, r):
        return W[m + N0, r] * R[src, m + N0, c, r]

    def finisher(own):
        def finish(m, c, r, k):
            old = R[src, m + N0, c, r]
            R[dst, m + N0, c, r] = old - k
            if own:
                U[m, c, r] = U[m, c, r] + W[m + N0, r] * old

        return finish

    y_stage(sm, get, lo - 1)
    stress_step(sm, st, LM, lo - 1, get)
    stress_step(sm, st, LM, lo, get)

    for m in range(lo, hi):
        stress_step(sm, st, LM, m + 1, get)
        node_step(st, m, finisher(0 <= m < OWN))
    node_step(st, hi, finisher(0 <= hi < OWN))


def materials(LM, mod, load, m):
    for r in range(4):
        v = load(r)
        one, two = v == 1, v == 2
        for i in range(2):
            LM[m + L0, i, r] = jnp.where(two, mod[3 * i + 2], jnp.where(one, mod[3 * i + 1], mod[3 * i]))


def raw(ref, k):
    return lambda r: load_raw(ref, (k,), r)


def weights(W, LM, lo, hi):
    for m in range(lo, hi + 1):
        t = []
        for r in range(4):
            v = (LM[m - 1 + L0, 0, r] + LM[m + L0, 0, r]) + 4.0 * (LM[m - 1 + L0, 1, r] + LM[m + L0, 1, r])
            t.append(v)
        for r in range(4):
            v = t[r] + x_prev(t, r)
            W[m + N0, r] = 0.5 / (v + y_prev(v))


def sign_of(par):
    return (1 - 2 * par[0]).astype(jnp.float32)


def oriented(v, c, sign):
    return v * sign if c == 2 else v


def kernel_prep(par, mod_h, u_h, f_h, ph_h, PB, UV, FV, MOD, ph, mod, sem):
    odd = par[0]
    copies = [
        pltpu.make_async_copy(src, dst, sem.at[i])
        for i, (src, dst) in enumerate(((ph_h, ph), (u_h, UV), (mod_h, mod), (f_h, FV)))
    ]
    for copy in copies:
        copy.start()
    copies[0].wait()
    for k in range(4):
        PB[3 + k] = ph[k].astype(jnp.float32)
    copies[1].wait()
    for c in range(3):
        PB[c] = UV[3 * odd, c]
    copies[2].wait()
    for i in range(2):
        for j in range(3):
            MOD[3 * i + j] = jnp.full((8, 256), mod[i, j] * 0.0625, jnp.float32)
    copies[3].wait()


def kernel_own(par, mod, u, f, own, R, LM, U, PAY, sm, st):
    odd, sign = par[0], sign_of(par)
    plane = lambda m: jnp.where(odd == 1, 3 - m, m)
    for k in range(4):
        materials(LM, mod, raw(own, 3 + k), jnp.where(odd == 1, 2 - k, k))
    for m in range(4):
        for c in range(3):
            for r in range(4):
                U[m, c, r] = oriented(load_raw(u, (plane(m), c), r), c, sign)

    def get(m, c, r):
        return U[m, c, r]

    def finish(m, c, r, k):
        v = oriented(load_raw(f, (plane(m), c), r), c, sign) - k
        R[0, m + N0, c, r] = v
        PAY[m, c, r] = v

    y_stage(sm, get, 0)
    stress_step(sm, st, LM, 0, get)
    for m in range(3):
        if m < 2:
            stress_step(sm, st, LM, m + 1, get)
        node_step(st, m, finish, below=m > 0)


def kernel_rest(par, mod, f, own, ua, pa, r_in, lm_in, u_in, p_in, R, LM, U, PAY, uw, sm, st):
    odd, sign = par[0], sign_of(par)
    for k in range(4):
        materials(LM, mod, raw(pa, k), jnp.where(odd == 1, 6 - k, 4 + k))
    for c in range(3):
        for r in range(4):
            uw[0, c, r] = oriented(load_raw(ua, (3 * odd, c), r), c, sign)
    for j in range(3):
        for r in range(4):
            v = load_raw(pa, (jnp.where(odd == 1, 3 - j, max(j - 1, 0)),), r).astype(jnp.float32)
            if j == 0:
                v = jnp.where(odd == 1, v, load_raw(own, (6,), r))
            PAY[4, j, r] = v

    def get(m, c, r):
        return U[m, c, r] if m < 4 else uw[0, c, r]

    def finish(m, c, r, k):
        v = oriented(load_raw(f, (jnp.where(odd == 1, 0, 3), c), r), c, sign) - k
        R[0, m + N0, c, r] = v
        PAY[m, c, r] = v

    y_stage(sm, get, 2)
    stress_step(sm, st, LM, 2, get)
    stress_step(sm, st, LM, 3, get)
    node_step(st, 3, finish)


def kernel_setup(par, mod, pb, r_in, lm_in, u_in, R, LM, U, W, EDGE, uw, sm, st):
    odd, sign = par[0], sign_of(par)
    for c in range(3):
        for r in range(4):
            uw[0, c, r] = oriented(load_raw(pb, (c,), r), c, sign)
    for k in range(4):
        materials(LM, mod, raw(pb, 3 + k), jnp.where(odd == 1, -2 - k, k - 4))
    weights(W, LM, -3, 6)

    def get(m, c, r):
        return uw[0, c, r] if m == -1 else U[0, c, r]

    def keep(m, c, r, k):
        EDGE[c, r] = k

    def take(m, c, r, k):
        R[0, N0, c, r] = R[0, N0, c, r] - k

    y_stage(sm, get, -1)
    stress_step(sm, st, LM, -1, get)
    node_step(st, -1, keep, below=False)
    node_step(st, 0, take, above=False)


def kernel_near(a2, r_in, lm_in, u_in, w_in, R, LM, U, W, sm, st):
    for j in range(3):
        for c in range(3):
            v = a2[3 - j, c]
            R[0, 4 + j + N0, c] = -v if c == 2 else v
    refs = (R, W, LM, U, sm, st)
    advance(refs, 0, 1, 5)
    advance(refs, 1, 2, 4)
    advance(refs, 2, 3, 3)


def kernel_mid(mod, b2, edge, r_in, lm_in, u_in, w_in, R, LM, U, W, PAY, sm, st):
    for j in range(4):
        for c in range(3):
            v = b2[j, c]
            v = -v if c == 2 else v
            R[0, -1 - j + N0, c] = v - edge[c] if j == 0 else v
    for j in range(3):
        materials(LM, mod, lambda r: b2[4, j, r], -5 - j)
    weights(W, LM, -6, -4)
    refs = (R, W, LM, U, sm, st)
    advance(refs, 0, -3, 0)
    advance(refs, 1, -2, 1)
    advance(refs, 2, -1, 2)
    for j in range(3):
        for c in range(3):
            PAY[j, c] = R[1, 1 + j + N0, c]


def kernel_lead(r_in, lm_in, u_in, w_in, R, LM, U, W, sm, st):
    refs = (R, W, LM, U, sm, st)
    advance(refs, 3, 0, 2)
    advance(refs, 4, 1, 1)


def kernel_inner(a3, r_in, lm_in, u_in, w_in, R, LM, U, W, sm, st):
    for j in range(3):
        for c in range(3):
            v = a3[2 - j, c]
            R[1, 4 + j + N0, c] = -v if c == 2 else v
    refs = (R, W, LM, U, sm, st)
    advance(refs, 3, 3, 5)
    advance(refs, 4, 2, 4)
    advance(refs, 5, 2, 3)


def kernel_last(par, b3, r_in, lm_in, u_in, w_in, sol_h, res_h, R, LM, U, W, sm, st, sol, res, sem):
    odd, sign = par[0], sign_of(par)

    def put(m):
        k = jnp.where(odd == 1, 3 - m, m)
        for c in range(3):
            for r in range(4):
                store_raw(sol, (m, c), r, oriented(U[m, c, r], c, sign))
                store_raw(res, (m, c), r, oriented(R[0, m + N0, c, r], c, sign))
        copies = [
            pltpu.make_async_copy(src.at[m], dst.at[k], sem.at[2 * m + i])
            for i, (src, dst) in enumerate(((sol, sol_h), (res, res_h)))
        ]
        for copy in copies:
            copy.start()
        return copies

    started = put(2) + put(3)
    for j in range(2):
        for c in range(3):
            R[0, -5 - j + N0, c] = b3[1 - j, c]
    refs = (R, W, LM, U, sm, st)
    advance(refs, 0, -5, -4)
    advance(refs, 1, -4, -3)
    advance(refs, 2, -3, -2)
    advance(refs, 3, -2, -1)
    advance(refs, 4, -1, 0)
    advance(refs, 5, 0, 1)
    started = started + put(0) + put(1)
    for copy in started:
        copy.wait()


def call(kernel, in_specs, out_shape, scratch, alias, planes, extra=(), out_specs=None):
    return pl.pallas_call(
        kernel,
        out_shape=out_shape,
        in_specs=in_specs,
        out_specs=out_specs or tuple(VMEM for _ in out_shape),
        scratch_shapes=[pltpu.VMEM(s + ROW, jnp.float32) for s in scratch] + list(extra),
        input_output_aliases=alias,
        compiler_params=pltpu.CompilerParams(vmem_limit_bytes=14 << 20),
        cost_estimate=pl.CostEstimate(flops=planes * 700000, bytes_accessed=planes * 500000, transcendentals=0),
    )


def tiles(x):
    lead = x.shape[:-2]
    return x.reshape(lead + (4, 8, 2, 128)).swapaxes(-3, -2).reshape(lead + (64, 128))


def untiles(x):
    lead = x.shape[:-2]
    return x.reshape(lead + (4, 2, 8, 128)).swapaxes(-3, -2).reshape(lead + (32, 256))


def sweeps(displacement, load, phase, moduli):
    count = lax.axis_size("slab")
    odd = lax.bitwise_and(lax.axis_index("slab"), 1)
    par = odd.reshape(1).astype(jnp.int32)
    inside = [(i, i ^ 1) for i in range(count)]
    across = [(i, (i - 1) % count if i % 2 == 0 else (i + 1) % count) for i in range(count)]

    def send(v, pairs):
        return lax.ppermute(v, "slab", pairs)

    sm, st = (LAYERS, 6), (LAYERS, 6)
    R, LM, U, W = f32(2, NODES, 3), f32(LAYERS, 2), f32(OWN, 3), f32(NODES)
    state = (R, LM, U, W)
    dma = lambda n: pltpu.SemaphoreType.DMA((n,))
    block = lambda n, kind=jnp.float32: pltpu.VMEM((n, 64, 128), kind)
    shape = lambda n: jax.ShapeDtypeStruct((n, 64, 128), jnp.float32)
    in_hbm = lambda v: pltpu.with_memory_space_constraint(v, pltpu.HBM)
    u_t, f_t, ph_t = (in_hbm(tiles(v)) for v in (displacement, load, phase))
    moduli = in_hbm(moduli)

    ua = send(displacement, inside)
    pa = send(phase, inside)
    whole = jax.ShapeDtypeStruct((OWN, 3, 64, 128), jnp.float32)
    six = jax.ShapeDtypeStruct((6, 8, 256), jnp.float32)
    pb0, uv, fv, mod = call(
        kernel_prep,
        [SMEM] + [HBM] * 4,
        (shape(7), whole, whole, six),
        [],
        {},
        2,
        [block(4, jnp.int32), pltpu.SMEM((2, 3), jnp.float32), dma(4)],
    )(par, moduli, u_t, f_t, ph_t)
    pb = send(pb0, across)
    r, lm, u, pay = call(
        kernel_own, [SMEM] + [VMEM] * 4, (R, LM, U, f32(5, 3)), [sm, st], {}, 4
    )(par, mod, uv, fv, pb0)
    r, lm, u, pay = call(
        kernel_rest,
        [SMEM] + [VMEM] * 9,
        (R, LM, U, f32(5, 3)),
        [(1, 3), sm, st],
        {6: 0, 7: 1, 8: 2, 9: 3},
        2,
    )(par, mod, fv, pb0, tiles(ua), tiles(pa), r, lm, u, pay)
    b2 = send(pay, across)
    a2 = send(pay, inside)
    r, lm, u, w, edge = call(
        kernel_setup,
        [SMEM] + [VMEM] * 5,
        state + (f32(3),),
        [(1, 3), sm, st],
        {3: 0, 4: 1, 5: 2},
        4,
    )(par, mod, pb, r, lm, u)
    r, lm, u, w = call(
        kernel_near, [VMEM] * 5, state, [sm, st], {1: 0, 2: 1, 3: 2, 4: 3}, 11
    )(a2, r, lm, u, w)
    b3 = send(a2[2:4], across)
    r, lm, u, w, pay = call(
        kernel_mid, [VMEM] * 7, state + (f32(3, 3),), [sm, st], {3: 0, 4: 1, 5: 2, 6: 3}, 14
    )(mod, b2, edge, r, lm, u, w)
    a3 = send(pay, inside)
    r, lm, u, w = call(
        kernel_lead, [VMEM] * 4, state, [sm, st], {0: 0, 1: 1, 2: 2, 3: 3}, 6
    )(r, lm, u, w)
    r, lm, u, w = call(
        kernel_inner, [VMEM] * 5, state, [sm, st], {1: 0, 2: 1, 3: 2, 4: 3}, 10
    )(a3, r, lm, u, w)
    sol, res, _, _, _, _ = call(
        kernel_last,
        [SMEM] + [VMEM] * 5,
        (whole, whole) + state,
        [sm, st],
        {2: 2, 3: 3, 4: 4, 5: 5},
        18,
        [pltpu.VMEM((OWN, 3, 64, 128), jnp.float32)] * 2 + [dma(8)],
        (HBM, HBM) + (VMEM,) * 4,
    )(par, b3, r, lm, u, w)
    return untiles(sol), untiles(res)


def solution(mesh):
    in_specs = (
        P("slab", None, "rve", None),
        P("slab", None, "rve", None),
        P("slab", "rve", None),
        P(),
    )
    out_specs = (P("slab", None, "rve", None), P("slab", None, "rve", None))
    return jax.shard_map(sweeps, mesh=mesh, in_specs=in_specs, out_specs=out_specs, check_vma=False)
```

```python
import jax
import jax.numpy as jnp
from jax import lax
from jax.experimental import pallas as pl
from jax.experimental.pallas import tpu as pltpu
from jax.sharding import PartitionSpec as P


OWN = 4
DEPTH = 6
INNER = 3
NODES = DEPTH + OWN + INNER
LAYERS = 16
N0 = DEPTH
L0 = 8

VMEM = pl.BlockSpec(memory_space=pltpu.VMEM)
SMEM = pl.BlockSpec(memory_space=pltpu.SMEM)
HBM = pl.BlockSpec(memory_space=pltpu.HBM)
ROW = (4, 8, 256)


def f32(*shape):
    return jax.ShapeDtypeStruct(shape + ROW, jnp.float32)


def even_rows():
    return lax.broadcasted_iota(jnp.int32, (8, 128), 0) % 2 == 0


def load_raw(ref, index, r):
    a = ref[index + (pl.ds(r, 8, stride=8), slice(None))]
    b = ref[index + (pl.ds(r + 4, 8, stride=8), slice(None))]
    even = even_rows()
    low = jnp.where(even, a, pltpu.roll(b, 1, 0))
    high = jnp.where(even, pltpu.roll(a, 7, 0), b)
    return jnp.concatenate([low, high], axis=1)


def store_raw(ref, index, r, value):
    low, high = value[:, :128], value[:, 128:]
    even = even_rows()
    ref[index + (pl.ds(r, 8, stride=8), slice(None))] = jnp.where(even, low, pltpu.roll(high, 1, 0))
    ref[index + (pl.ds(r + 4, 8, stride=8), slice(None))] = jnp.where(even, pltpu.roll(low, 7, 0), high)


def y_next(v):
    return pltpu.roll(v, 255, 1)


def y_prev(v):
    return pltpu.roll(v, 1, 1)


def x_prev(rows, r):
    return rows[r - 1] if r > 0 else pltpu.roll(rows[3], 1, 0)


def y_stage(sm, get, m):
    for c in range(3):
        for r in range(4):
            d = get(m, c, r)
            n = y_next(d)
            sm[m + L0, c, r] = d + n
            sm[m + L0, 3 + c, r] = n - d


def stress_step(sm, st, lm, m, get, save=None):
    first = prev = None

    def stress(z, nxt, r):
        x0, y1, z2, _, _, e, pd, qd = z
        gxx = nxt[0] - x0
        gyy = nxt[1] + y1
        gzz = nxt[2] + z2
        lame, mu = lm[m + L0, 0, r], lm[m + L0, 1, r]
        lt = lame * (gxx + gyy + gzz)
        mu2 = mu + mu
        values = (
            lt + mu2 * gxx,
            mu * (nxt[3] + pd),
            lt + mu2 * gyy,
            mu * (nxt[4] + qd),
            mu * (nxt[5] + e),
            lt + mu2 * gzz,
        )
        for i, v in enumerate(values):
            st[m + L0, i, r] = v
            if save is not None:
                save[i, r] = v

    for r in range(4):
        s, my, j = [], [], []
        for c in range(3):
            d = get(m + 1, c, r)
            n = y_next(d)
            su, mu_ = d + n, n - d
            sl, ml = sm[m + L0, c, r], sm[m + L0, 3 + c, r]
            sm[m + 1 + L0, c, r] = su
            sm[m + 1 + L0, 3 + c, r] = mu_
            s.append(sl + su)
            my.append(ml + mu_)
            j.append(su - sl)
        z = (s[0], my[1], j[2], my[0] + s[1], j[0] + s[2], j[1] + my[2], my[0] - s[1], j[0] - s[2])
        if r == 0:
            first = z
        else:
            stress(prev, z, r - 1)
        prev = z
    stress(prev, tuple(pltpu.roll(v, 7, 0) for v in first[:6]), 3)


def node_sums(st, m, r, above, below, top):
    upper = st.at[m + L0] if top is None else top
    new = [upper[i, r] if above else None for i in range(6)]
    old = [st[m - 1 + L0, i, r] if below else None for i in range(6)]

    def plus(i):
        return new[i] if not below else old[i] if not above else new[i] + old[i]

    def minus(i):
        return -new[i] if not below else old[i] if not above else old[i] - new[i]

    xx, xy, yy, xz, yz = (plus(i) for i in range(5))
    dxz, dyz, dzz = (minus(i) for i in range(3, 6))
    return (
        (xx + dxz, xy + dyz, xz + dzz),
        (dxz - xx, dyz - xy, dzz - xz),
        (xy, yy, yz),
    )


def node_step(st, m, finish, above=True, below=True, top=None):
    first = prev = None

    def out(pq, pp, ph, r):
        for c in range(3):
            g = pp[c] + pq[1][c]
            hh = ph[c] + pq[2][c]
            finish(m, c, r, (g - hh) + y_prev(g + hh))

    for r in range(4):
        pq = node_sums(st, m, r, above, below, top)
        if r == 0:
            first = pq
        else:
            out(pq, prev[0], prev[2], r)
        prev = pq
    roll = lambda v: pltpu.roll(v, 1, 0)
    out(first, tuple(map(roll, prev[0])), tuple(map(roll, prev[2])), 0)


def advance(refs, s, lo, hi, save=None, top=None):
    R, W, LM, U, sm, st = refs
    src, dst = s % 2, (s + 1) % 2

    def get(m, c, r):
        return W[m + N0, r] * R[src, m + N0, c, r]

    def finisher(own):
        def finish(m, c, r, k):
            old = R[src, m + N0, c, r]
            R[dst, m + N0, c, r] = old - k
            if own:
                U[m, c, r] = U[m, c, r] + W[m + N0, r] * old

        return finish

    def layer(m):
        if m < hi or (m == hi and top is None):
            stress_step(sm, st, LM, m, get)

    y_stage(sm, get, lo - 1)
    stress_step(sm, st, LM, lo - 1, get, save)
    layer(lo)
    for m in range(lo, hi + 1):
        layer(m + 1)
        node_step(st, m, finisher(0 <= m < OWN), top=top if m == hi else None)


def materials(LM, mod, load, m):
    for r in range(4):
        v = load(r)
        one, two = v == 1, v == 2
        for i in range(2):
            LM[m + L0, i, r] = jnp.where(two, mod[3 * i + 2], jnp.where(one, mod[3 * i + 1], mod[3 * i]))


def raw(ref, k):
    return lambda r: load_raw(ref, (k,), r)


def weights(W, LM, lo, hi):
    for m in range(lo, hi + 1):
        t = []
        for r in range(4):
            v = (LM[m - 1 + L0, 0, r] + LM[m + L0, 0, r]) + 4.0 * (LM[m - 1 + L0, 1, r] + LM[m + L0, 1, r])
            t.append(v)
        for r in range(4):
            v = t[r] + x_prev(t, r)
            W[m + N0, r] = 0.5 / (v + y_prev(v))


def sign_of(par):
    return (1 - 2 * par[0]).astype(jnp.float32)


def oriented(v, c, sign):
    return v * sign if c == 2 else v


def kernel_own(par, mod_h, u_h, f_h, ph_h, R, LM, U, PA, B1, MOD, F3, sm, st, u, f, ph, mod, sem):
    odd, sign = par[0], sign_of(par)
    copies = [
        pltpu.make_async_copy(src, dst, sem.at[i])
        for i, (src, dst) in enumerate(((mod_h, mod), (ph_h, ph), (u_h, u), (f_h, f)))
    ]
    for copy in copies:
        copy.start()
    plane = lambda m: jnp.where(odd == 1, 3 - m, m)
    copies[0].wait()
    for i in range(2):
        for j in range(3):
            MOD[3 * i + j] = jnp.full((8, 256), mod[i, j] * 0.0625, jnp.float32)
    copies[1].wait()
    for k in range(4):
        for r in range(4):
            B1[3 + k, r] = load_raw(ph, (k,), r).astype(jnp.float32)
        materials(LM, MOD, lambda r: B1[3 + k, r], jnp.where(odd == 1, 2 - k, k))
    copies[2].wait()
    for m in range(4):
        for c in range(3):
            for r in range(4):
                v = oriented(load_raw(u, (plane(m), c), r), c, sign)
                U[m, c, r] = v
                if m == 0:
                    B1[c, r] = v

    def get(m, c, r):
        return U[m, c, r]

    def finish(m, c, r, k):
        v = oriented(load_raw(f, (plane(m), c), r), c, sign) - k
        R[0, m + N0, c, r] = v
        B1[7 + 3 * m + c, r] = v
        if m > 0:
            PA[m - 1, c, r] = v

    y_stage(sm, get, 0)
    stress_step(sm, st, LM, 0, get)
    stress_step(sm, st, LM, 1, get)
    copies[3].wait()
    for c in range(3):
        for r in range(4):
            F3[c, r] = oriented(load_raw(f, (plane(3), c), r), c, sign)
    node_step(st, 0, finish, below=False)
    stress_step(sm, st, LM, 2, get)
    node_step(st, 1, finish)
    node_step(st, 2, finish)


def kernel_rest(par, mod, f3, b1, ua, pa, r_in, lm_in, u_in, p_in, R, LM, U, PA, P3, uw, sm, st):
    odd, sign = par[0], sign_of(par)
    for k in range(4):
        materials(LM, mod, raw(pa, k), jnp.where(odd == 1, 6 - k, 4 + k))
    for c in range(3):
        for r in range(4):
            uw[0, c, r] = oriented(load_raw(ua, (3 * odd, c), r), c, sign)
    for j in range(3):
        for r in range(4):
            v = load_raw(pa, (jnp.where(odd == 1, 3 - j, max(j - 1, 0)),), r).astype(jnp.float32)
            P3[3, j, r] = jnp.where(odd == 1, v, b1[6, r]) if j == 0 else v

    def get(m, c, r):
        return U[m, c, r] if m < 4 else uw[0, c, r]

    def finish(m, c, r, k):
        v = f3[c, r] - k
        R[0, m + N0, c, r] = v
        PA[2, c, r] = v
        P3[0, c, r] = v

    y_stage(sm, get, 2)
    stress_step(sm, st, LM, 2, get)
    stress_step(sm, st, LM, 3, get)
    node_step(st, 3, finish)


def flipped(v, c):
    return -v if c == 2 else v


def kernel_pack(a2, p_in, P3):
    for j in range(2):
        for c in range(3):
            P3[1 + j, c] = flipped(a2[2 - j, c], c)


def kernel_near(a2, r_in, lm_in, u_in, R, LM, U, W, EN, sm, st):
    for j in range(3):
        for c in range(3):
            R[0, 4 + j + N0, c] = flipped(a2[2 - j, c], c)
    weights(W, LM, 1, 6)
    refs = (R, W, LM, U, sm, st)
    advance(refs, 0, 2, 5, EN.at[0])
    advance(refs, 1, 3, 4, EN.at[1])


def kernel_mid(par, mod, b1, en, r_in, lm_in, u_in, w_in, R, LM, U, W, ES, PAY, edge, sm, st):
    odd = par[0]
    for k in range(4):
        materials(LM, mod, lambda r: b1[3 + k, r], jnp.where(odd == 1, -2 - k, k - 4))
    weights(W, LM, -3, 0)

    def get(m, c, r):
        return flipped(b1[c, r], c) if m == -1 else U[0, c, r]

    def keep(m, c, r, k):
        edge[c, r] = k

    def take(m, c, r, k):
        R[0, N0, c, r] = R[0, N0, c, r] - k

    y_stage(sm, get, -1)
    stress_step(sm, st, LM, -1, get)
    node_step(st, -1, keep, below=False)
    node_step(st, 0, take, above=False)
    for j in range(3):
        for c in range(3):
            for r in range(4):
                v = flipped(b1[7 + 3 * j + c, r], c)
                R[0, -1 - j + N0, c, r] = v - edge[c, r] if j == 0 else v
    refs = (R, W, LM, U, sm, st)
    advance(refs, 0, -2, 1, ES.at[0], en.at[0])
    advance(refs, 1, -1, 2, ES.at[1], en.at[1])
    advance(refs, 2, 0, 3, ES.at[2])
    for j in range(3):
        for c in range(3):
            PAY[j, c] = R[1, 1 + j + N0, c]


def kernel_lead(r_in, lm_in, u_in, w_in, e_in, R, LM, U, W, ES, sm, st):
    advance((R, W, LM, U, sm, st), 3, 1, 2, ES.at[3])


def kernel_inner(a3, r_in, lm_in, u_in, w_in, e_in, R, LM, U, W, ES, sm, st):
    for j in range(3):
        for c in range(3):
            R[1, 4 + j + N0, c] = flipped(a3[2 - j, c], c)
    refs = (R, W, LM, U, sm, st)
    advance(refs, 3, 3, 5)
    advance(refs, 4, 2, 4, ES.at[4])
    advance(refs, 5, 3, 3, ES.at[5])


def kernel_last(par, mod, b3, es, r_in, lm_in, u_in, w_in, sol_h, res_h, R, LM, U, W, sm, st, sol, res, sem):
    odd, sign = par[0], sign_of(par)

    def put(m):
        k = jnp.where(odd == 1, 3 - m, m)
        for c in range(3):
            for r in range(4):
                store_raw(sol, (m, c), r, oriented(U[m, c, r], c, sign))
                store_raw(res, (m, c), r, oriented(R[0, m + N0, c, r], c, sign))
        copies = [
            pltpu.make_async_copy(src.at[m], dst.at[k], sem.at[2 * m + i])
            for i, (src, dst) in enumerate(((sol, sol_h), (res, res_h)))
        ]
        for copy in copies:
            copy.start()
        return copies

    started = put(3)
    for j in range(3):
        materials(LM, mod, lambda r: b3[3, j, r], -5 - j)
    weights(W, LM, -6, -4)
    for j in range(3):
        for c in range(3):
            R[0, -4 - j + N0, c] = flipped(b3[j, c], c)
    refs = (R, W, LM, U, sm, st)
    advance(refs, 0, -5, -3, top=es.at[0])
    advance(refs, 1, -4, -2, top=es.at[1])
    advance(refs, 2, -3, -1, top=es.at[2])
    advance(refs, 3, -2, 0, top=es.at[3])
    advance(refs, 4, -1, 1, top=es.at[4])
    advance(refs, 5, 0, 2, top=es.at[5])
    for m in range(3):
        started = started + put(m)
    for copy in started:
        copy.wait()


def call(kernel, in_specs, out_shape, scratch, alias, planes, extra=(), out_specs=None):
    return pl.pallas_call(
        kernel,
        out_shape=out_shape,
        in_specs=in_specs,
        out_specs=out_specs or tuple(VMEM for _ in out_shape),
        scratch_shapes=[pltpu.VMEM(s + ROW, jnp.float32) for s in scratch] + list(extra),
        input_output_aliases=alias,
        compiler_params=pltpu.CompilerParams(vmem_limit_bytes=14 << 20),
        cost_estimate=pl.CostEstimate(flops=planes * 700000, bytes_accessed=planes * 500000, transcendentals=0),
    )


def tiles(x):
    lead = x.shape[:-2]
    return x.reshape(lead + (4, 8, 2, 128)).swapaxes(-3, -2).reshape(lead + (64, 128))


def untiles(x):
    lead = x.shape[:-2]
    return x.reshape(lead + (4, 2, 8, 128)).swapaxes(-3, -2).reshape(lead + (32, 256))


def sweeps(displacement, load, phase, moduli):
    count = lax.axis_size("slab")
    odd = lax.bitwise_and(lax.axis_index("slab"), 1)
    par = odd.reshape(1).astype(jnp.int32)
    inside = [(i, i ^ 1) for i in range(count)]
    across = [(i, (i - 1) % count if i % 2 == 0 else (i + 1) % count) for i in range(count)]

    def send(v, pairs):
        return lax.ppermute(v, "slab", pairs)

    sm, st = (LAYERS, 6), (LAYERS, 6)
    R, LM, U, W = f32(2, NODES, 3), f32(LAYERS, 2), f32(OWN, 3), f32(NODES)
    state = (R, LM, U, W)
    dma = lambda n: pltpu.SemaphoreType.DMA((n,))
    block = lambda n, kind=jnp.float32: pltpu.VMEM((n, 64, 128), kind)
    in_hbm = lambda v: pltpu.with_memory_space_constraint(v, pltpu.HBM)
    u_t, f_t, ph_t = (in_hbm(tiles(v)) for v in (displacement, load, phase))
    moduli = in_hbm(moduli)

    whole = jax.ShapeDtypeStruct((OWN, 3, 64, 128), jnp.float32)
    six = jax.ShapeDtypeStruct((6, 8, 256), jnp.float32)
    fields = pltpu.VMEM((OWN, 3, 64, 128), jnp.float32)
    ua = send(displacement, inside)
    pa = send(phase, inside)
    r, lm, u, pay, pay1, mod, f3 = call(
        kernel_own,
        [SMEM] + [HBM] * 4,
        (R, LM, U, f32(3, 3), f32(16), six, f32(3)),
        [sm, st],
        {},
        4,
        [fields, fields, block(4, jnp.int32), pltpu.SMEM((2, 3), jnp.float32), dma(4)],
    )(par, moduli, u_t, f_t, ph_t)
    b1 = send(pay1, across)
    r, lm, u, pay, pay3 = call(
        kernel_rest,
        [SMEM] + [VMEM] * 9,
        (R, LM, U, f32(3, 3), f32(4, 3)),
        [(1, 3), sm, st],
        {6: 0, 7: 1, 8: 2, 9: 3},
        2,
    )(par, mod, f3, pay1, tiles(ua), tiles(pa), r, lm, u, pay)
    a2 = send(pay, inside)
    (pay3,) = call(kernel_pack, [VMEM] * 2, (f32(4, 3),), [], {1: 0}, 1)(a2, pay3)
    b3 = send(pay3, across)
    r, lm, u, w, en = call(
        kernel_near, [VMEM] * 4, state + (f32(2, 6),), [sm, st], {1: 0, 2: 1, 3: 2}, 8
    )(a2, r, lm, u)
    r, lm, u, w, es, pay = call(
        kernel_mid,
        [SMEM] + [VMEM] * 7,
        state + (f32(6, 6), f32(3, 3)),
        [(3,), sm, st],
        {4: 0, 5: 1, 6: 2, 7: 3},
        14,
    )(par, mod, b1, en, r, lm, u, w)
    a3 = send(pay, inside)
    r, lm, u, w, es = call(
        kernel_lead, [VMEM] * 5, state + (f32(6, 6),), [sm, st], {0: 0, 1: 1, 2: 2, 3: 3, 4: 4}, 3
    )(r, lm, u, w, es)
    r, lm, u, w, es = call(
        kernel_inner, [VMEM] * 6, state + (f32(6, 6),), [sm, st], {1: 0, 2: 1, 3: 2, 4: 3, 5: 4}, 9
    )(a3, r, lm, u, w, es)
    sol, res, _, _, _, _ = call(
        kernel_last,
        [SMEM] + [VMEM] * 7,
        (whole, whole) + state,
        [sm, st],
        {4: 2, 5: 3, 6: 4, 7: 5},
        24,
        [fields, fields, dma(8)],
        (HBM, HBM) + (VMEM,) * 4,
    )(par, mod, b3, es, r, lm, u, w)
    return untiles(sol), untiles(res)


def solution(mesh):
    in_specs = (
        P("slab", None, "rve", None),
        P("slab", None, "rve", None),
        P("slab", "rve", None),
        P(),
    )
    out_specs = (P("slab", None, "rve", None), P("slab", None, "rve", None))
    return jax.shard_map(sweeps, mesh=mesh, in_specs=in_specs, out_specs=out_specs, check_vma=False)
```

```python
import jax
import jax.numpy as jnp
from jax import lax
from jax.experimental import pallas as pl
from jax.experimental.pallas import tpu as pltpu
from jax.sharding import PartitionSpec as P


OWN = 4
DEPTH = 6
INNER = 3
NODES = DEPTH + OWN + INNER
LAYERS = 16
N0 = DEPTH
L0 = 8

VMEM = pl.BlockSpec(memory_space=pltpu.VMEM)
SMEM = pl.BlockSpec(memory_space=pltpu.SMEM)
HBM = pl.BlockSpec(memory_space=pltpu.HBM)
ROW = (4, 8, 256)


def f32(*shape):
    return jax.ShapeDtypeStruct(shape + ROW, jnp.float32)


def even_rows():
    return lax.broadcasted_iota(jnp.int32, (8, 128), 0) % 2 == 0


def load_raw(ref, index, r):
    a = ref[index + (pl.ds(r, 8, stride=8), slice(None))]
    b = ref[index + (pl.ds(r + 4, 8, stride=8), slice(None))]
    even = even_rows()
    low = jnp.where(even, a, pltpu.roll(b, 1, 0))
    high = jnp.where(even, pltpu.roll(a, 7, 0), b)
    return jnp.concatenate([low, high], axis=1)


def store_raw(ref, index, r, value):
    low, high = value[:, :128], value[:, 128:]
    even = even_rows()
    ref[index + (pl.ds(r, 8, stride=8), slice(None))] = jnp.where(even, low, pltpu.roll(high, 1, 0))
    ref[index + (pl.ds(r + 4, 8, stride=8), slice(None))] = jnp.where(even, pltpu.roll(low, 7, 0), high)


def y_next(v):
    return pltpu.roll(v, 255, 1)


def y_prev(v):
    return pltpu.roll(v, 1, 1)


def x_prev(rows, r):
    return rows[r - 1] if r > 0 else pltpu.roll(rows[3], 1, 0)


def y_stage(sm, get, m):
    for c in range(3):
        for r in range(4):
            d = get(m, c, r)
            n = y_next(d)
            sm[m + L0, c, r] = d + n
            sm[m + L0, 3 + c, r] = n - d


def stress_step(sm, st, lm, m, get, save=None):
    first = prev = None

    def stress(z, nxt, r):
        x0, y1, z2, _, _, e, pd, qd = z
        gxx = nxt[0] - x0
        gyy = nxt[1] + y1
        gzz = nxt[2] + z2
        lame, mu = lm[m + L0, 0, r], lm[m + L0, 1, r]
        lt = lame * (gxx + gyy + gzz)
        mu2 = mu + mu
        values = (
            lt + mu2 * gxx,
            mu * (nxt[3] + pd),
            lt + mu2 * gyy,
            mu * (nxt[4] + qd),
            mu * (nxt[5] + e),
            lt + mu2 * gzz,
        )
        for i, v in enumerate(values):
            st[m + L0, i, r] = v
            if save is not None:
                save[i, r] = v

    for r in range(4):
        s, my, j = [], [], []
        for c in range(3):
            d = get(m + 1, c, r)
            n = y_next(d)
            su, mu_ = d + n, n - d
            sl, ml = sm[m + L0, c, r], sm[m + L0, 3 + c, r]
            sm[m + 1 + L0, c, r] = su
            sm[m + 1 + L0, 3 + c, r] = mu_
            s.append(sl + su)
            my.append(ml + mu_)
            j.append(su - sl)
        z = (s[0], my[1], j[2], my[0] + s[1], j[0] + s[2], j[1] + my[2], my[0] - s[1], j[0] - s[2])
        if r == 0:
            first = z
        else:
            stress(prev, z, r - 1)
        prev = z
    stress(prev, tuple(pltpu.roll(v, 7, 0) for v in first[:6]), 3)


def node_sums(st, m, r, above, below, top):
    upper = st.at[m + L0] if top is None else top
    new = [upper[i, r] if above else None for i in range(6)]
    old = [st[m - 1 + L0, i, r] if below else None for i in range(6)]

    def plus(i):
        return new[i] if not below else old[i] if not above else new[i] + old[i]

    def minus(i):
        return -new[i] if not below else old[i] if not above else old[i] - new[i]

    xx, xy, yy, xz, yz = (plus(i) for i in range(5))
    dxz, dyz, dzz = (minus(i) for i in range(3, 6))
    return (
        (xx + dxz, xy + dyz, xz + dzz),
        (dxz - xx, dyz - xy, dzz - xz),
        (xy, yy, yz),
    )


def node_step(st, m, finish, above=True, below=True, top=None):
    first = prev = None

    def out(pq, pp, ph, r):
        for c in range(3):
            g = pp[c] + pq[1][c]
            hh = ph[c] + pq[2][c]
            finish(m, c, r, (g - hh) + y_prev(g + hh))

    for r in range(4):
        pq = node_sums(st, m, r, above, below, top)
        if r == 0:
            first = pq
        else:
            out(pq, prev[0], prev[2], r)
        prev = pq
    roll = lambda v: pltpu.roll(v, 1, 0)
    out(first, tuple(map(roll, prev[0])), tuple(map(roll, prev[2])), 0)


def advance(refs, s, lo, hi, save=None, top=None, after=None):
    R, W, LM, U, sm, st = refs
    src, dst = s % 2, (s + 1) % 2

    def get(m, c, r):
        return W[m + N0, r] * R[src, m + N0, c, r]

    def finisher(own):
        def finish(m, c, r, k):
            old = R[src, m + N0, c, r]
            R[dst, m + N0, c, r] = old - k
            if own and after is None:
                U[m, c, r] = U[m, c, r] + W[m + N0, r] * old

        return finish

    def layer(m):
        if m < hi or (m == hi and top is None):
            stress_step(sm, st, LM, m, get)

    y_stage(sm, get, lo - 1)
    stress_step(sm, st, LM, lo - 1, get, save)
    layer(lo)
    for m in range(lo, hi + 1):
        layer(m + 1)
        node_step(st, m, finisher(0 <= m < OWN), top=top if m == hi else None)
        if after is not None:
            after(m)


def materials(LM, mod, load, m):
    for r in range(4):
        v = load(r)
        one, two = v == 1, v == 2
        for i in range(2):
            LM[m + L0, i, r] = jnp.where(two, mod[3 * i + 2], jnp.where(one, mod[3 * i + 1], mod[3 * i]))


def weights(W, LM, lo, hi):
    for m in range(lo, hi + 1):
        t = []
        for r in range(4):
            v = (LM[m - 1 + L0, 0, r] + LM[m + L0, 0, r]) + 4.0 * (LM[m - 1 + L0, 1, r] + LM[m + L0, 1, r])
            t.append(v)
        for r in range(4):
            v = t[r] + x_prev(t, r)
            W[m + N0, r] = 0.5 / (v + y_prev(v))


def sign_of(par):
    return (1 - 2 * par[0]).astype(jnp.float32)


def oriented(v, c, sign):
    return v * sign if c == 2 else v


def flipped(v, c):
    return -v if c == 2 else v


def kernel_own(par, mod_h, u_h, f_h, ph_h, R, LM, U, A1, B1, MOD, sm, st, u, f, ph, mod, sem):
    odd, sign = par[0], sign_of(par)
    copies = [
        pltpu.make_async_copy(src, dst, sem.at[i])
        for i, (src, dst) in enumerate(((mod_h, mod), (ph_h, ph), (u_h, u), (f_h, f)))
    ]
    for copy in copies:
        copy.start()
    plane = lambda m: jnp.where(odd == 1, 3 - m, m)
    copies[0].wait()
    for i in range(2):
        for j in range(3):
            MOD[3 * i + j] = jnp.full((8, 256), mod[i, j] * 0.0625, jnp.float32)
    copies[1].wait()
    for k in range(4):
        for r in range(4):
            v = load_raw(ph, (k,), r).astype(jnp.float32)
            A1[3 + k, r] = v
            B1[3 + k, r] = v
        materials(LM, MOD, lambda r: B1[3 + k, r], jnp.where(odd == 1, 2 - k, k))
    copies[2].wait()
    for m in range(4):
        for c in range(3):
            for r in range(4):
                v = oriented(load_raw(u, (plane(m), c), r), c, sign)
                U[m, c, r] = v
                if m == 0:
                    B1[c, r] = v
                if m == 3:
                    A1[c, r] = v

    def get(m, c, r):
        return U[m, c, r]

    def finish(m, c, r, k):
        v = oriented(load_raw(f, (plane(m), c), r), c, sign) - k
        R[0, m + N0, c, r] = v
        if m < 3:
            B1[7 + 3 * m + c, r] = v
        if m > 0:
            A1[7 + 3 * (3 - m) + c, r] = v

    y_stage(sm, get, 0)
    stress_step(sm, st, LM, 0, get)
    stress_step(sm, st, LM, 1, get)
    copies[3].wait()
    node_step(st, 0, finish, below=False)
    stress_step(sm, st, LM, 2, get)
    for m in range(1, 4):
        node_step(st, m, finish, above=m < 3)


def kernel_fin(par, mod, b1, a1, r_in, lm_in, u_in, R, LM, U, P3, sm, st):
    odd = par[0]
    for k in range(4):
        materials(LM, mod, lambda r: a1[3 + k, r], jnp.where(odd == 1, 6 - k, 4 + k))
    for j in range(3):
        for r in range(4):
            v = a1[3 + jnp.where(odd == 1, 3 - j, max(j - 1, 0)), r]
            P3[3, j, r] = jnp.where(odd == 1, v, b1[6, r]) if j == 0 else v
    for c in range(3):
        v = flipped(a1[10 + c], c)
        R[0, 5 + N0, c] = v
        P3[2, c] = v
        R[0, 6 + N0, c] = flipped(a1[13 + c], c)

    def get(m, c, r):
        return U[3, c, r] if m == 3 else flipped(a1[c, r], c)

    def finish(m, c, r, k):
        v = (R[0, 3 + N0, c, r] if m == 3 else flipped(a1[7 + c, r], c)) - k
        R[0, m + N0, c, r] = v
        P3[m - 3, c, r] = v

    y_stage(sm, get, 3)
    stress_step(sm, st, LM, 3, get)
    node_step(st, 3, finish, below=False)
    node_step(st, 4, finish, above=False)


def kernel_near(r_in, lm_in, u_in, R, LM, U, W, EN, sm, st):
    weights(W, LM, 1, 6)
    refs = (R, W, LM, U, sm, st)
    advance(refs, 0, 2, 5, EN.at[0])
    advance(refs, 1, 3, 4, EN.at[1])


def kernel_mid(par, mod, b1, en, r_in, lm_in, u_in, w_in, R, LM, U, W, E1, PAY, edge, sm, st):
    odd = par[0]
    for k in range(4):
        materials(LM, mod, lambda r: b1[3 + k, r], jnp.where(odd == 1, -2 - k, k - 4))
    weights(W, LM, -3, 0)

    def get(m, c, r):
        return flipped(b1[c, r], c) if m == -1 else U[0, c, r]

    def keep(m, c, r, k):
        edge[c, r] = k

    def take(m, c, r, k):
        R[0, N0, c, r] = R[0, N0, c, r] - k

    y_stage(sm, get, -1)
    stress_step(sm, st, LM, -1, get)
    node_step(st, -1, keep, below=False)
    node_step(st, 0, take, above=False)
    for j in range(3):
        for c in range(3):
            for r in range(4):
                v = flipped(b1[7 + 3 * j + c, r], c)
                R[0, -1 - j + N0, c, r] = v - edge[c, r] if j == 0 else v
    refs = (R, W, LM, U, sm, st)
    advance(refs, 0, -1, 1, E1.at[0], en.at[0])
    advance(refs, 1, 0, 2, E1.at[1], en.at[1])
    advance(refs, 2, 1, 3, E1.at[2])
    for j in range(3):
        for c in range(3):
            PAY[j, c] = R[1, 1 + j + N0, c]


def kernel_lead(e1, r_in, lm_in, u_in, w_in, R, LM, U, W, ES, sm, st):
    refs = (R, W, LM, U, sm, st)
    advance(refs, 0, -2, -2, ES.at[0], e1.at[0])
    advance(refs, 1, -1, -1, ES.at[1], e1.at[1])
    advance(refs, 2, 0, 0, ES.at[2], e1.at[2])
    advance(refs, 3, 1, 2, ES.at[3])


def kernel_inner(a3, r_in, lm_in, u_in, w_in, e_in, R, LM, U, W, ES, sm, st):
    for j in range(3):
        for c in range(3):
            R[1, 4 + j + N0, c] = flipped(a3[2 - j, c], c)
    refs = (R, W, LM, U, sm, st)
    advance(refs, 3, 3, 5)
    advance(refs, 4, 2, 4, ES.at[4])
    advance(refs, 5, 3, 3, ES.at[5])


def kernel_last(par, mod, b3, es, r_in, lm_in, u_in, w_in, sol_h, res_h, R, LM, U, W, sm, st, sol, res, sem):
    odd, sign = par[0], sign_of(par)
    started = []

    def put(buf, dst, i, m, get):
        for c in range(3):
            for r in range(4):
                store_raw(buf, (m, c), r, oriented(get(c, r), c, sign))
        copy = pltpu.make_async_copy(buf.at[m], dst.at[jnp.where(odd == 1, 3 - m, m)], sem.at[2 * m + i])
        copy.start()
        started.append(copy)

    def put_res(m):
        put(res, res_h, 1, m, lambda c, r: R[0, m + N0, c, r])

    put(sol, sol_h, 0, 3, lambda c, r: U[3, c, r])
    put_res(3)
    for j in range(3):
        materials(LM, mod, lambda r: b3[3, j, r], -5 - j)
    weights(W, LM, -6, -4)
    for j in range(3):
        for c in range(3):
            R[0, -4 - j + N0, c] = flipped(b3[j, c], c)
    refs = (R, W, LM, U, sm, st)
    for s in range(5):
        advance(refs, s, s - 5, s - 3, top=es.at[s])
    for m in range(3):
        put(sol, sol_h, 0, m, lambda c, r: U[m, c, r] + W[m + N0, r] * R[1, m + N0, c, r])
    advance(refs, 5, 0, 2, top=es.at[5], after=put_res)
    for copy in started:
        copy.wait()


def call(kernel, in_specs, out_shape, scratch, alias, planes, extra=(), out_specs=None):
    return pl.pallas_call(
        kernel,
        out_shape=out_shape,
        in_specs=in_specs,
        out_specs=out_specs or tuple(VMEM for _ in out_shape),
        scratch_shapes=[pltpu.VMEM(s + ROW, jnp.float32) for s in scratch] + list(extra),
        input_output_aliases=alias,
        compiler_params=pltpu.CompilerParams(vmem_limit_bytes=14 << 20),
        cost_estimate=pl.CostEstimate(flops=planes * 700000, bytes_accessed=planes * 500000, transcendentals=0),
    )


def tiles(x):
    lead = x.shape[:-2]
    return x.reshape(lead + (4, 8, 2, 128)).swapaxes(-3, -2).reshape(lead + (64, 128))


def untiles(x):
    lead = x.shape[:-2]
    return x.reshape(lead + (4, 2, 8, 128)).swapaxes(-3, -2).reshape(lead + (32, 256))


def sweeps(displacement, load, phase, moduli):
    count = lax.axis_size("slab")
    odd = lax.bitwise_and(lax.axis_index("slab"), 1)
    par = odd.reshape(1).astype(jnp.int32)
    inside = [(i, i ^ 1) for i in range(count)]
    across = [(i, (i - 1) % count if i % 2 == 0 else (i + 1) % count) for i in range(count)]

    def send(v, pairs):
        return lax.ppermute(v, "slab", pairs)

    sm, st = (LAYERS, 6), (LAYERS, 6)
    R, LM, U, W = f32(2, NODES, 3), f32(LAYERS, 2), f32(OWN, 3), f32(NODES)
    state = (R, LM, U, W)
    dma = lambda n: pltpu.SemaphoreType.DMA((n,))
    block = lambda n, kind=jnp.float32: pltpu.VMEM((n, 64, 128), kind)
    in_hbm = lambda v: pltpu.with_memory_space_constraint(v, pltpu.HBM)
    u_t, f_t, ph_t = (in_hbm(tiles(v)) for v in (displacement, load, phase))
    moduli = in_hbm(moduli)

    whole = jax.ShapeDtypeStruct((OWN, 3, 64, 128), jnp.float32)
    six = jax.ShapeDtypeStruct((6, 8, 256), jnp.float32)
    fields = pltpu.VMEM((OWN, 3, 64, 128), jnp.float32)
    r, lm, u, pay, pay1, mod = call(
        kernel_own,
        [SMEM] + [HBM] * 4,
        (R, LM, U, f32(16), f32(16), six),
        [sm, st],
        {},
        4,
        [fields, fields, block(4, jnp.int32), pltpu.SMEM((2, 3), jnp.float32), dma(4)],
    )(par, moduli, u_t, f_t, ph_t)
    b1 = send(pay1, across)
    a1 = send(pay, inside)
    r, lm, u, pay3 = call(
        kernel_fin, [SMEM] + [VMEM] * 6, (R, LM, U, f32(4, 3)), [sm, st], {4: 0, 5: 1, 6: 2}, 2
    )(par, mod, pay1, a1, r, lm, u)
    b3 = send(pay3, across)
    r, lm, u, w, en = call(
        kernel_near, [VMEM] * 3, state + (f32(2, 6),), [sm, st], {0: 0, 1: 1, 2: 2}, 8
    )(r, lm, u)
    r, lm, u, w, e1, pay = call(
        kernel_mid,
        [SMEM] + [VMEM] * 7,
        state + (f32(3, 6), f32(3, 3)),
        [(3,), sm, st],
        {4: 0, 5: 1, 6: 2, 7: 3},
        14,
    )(par, mod, b1, en, r, lm, u, w)
    a3 = send(pay, inside)
    r, lm, u, w, es = call(
        kernel_lead, [VMEM] * 5, state + (f32(6, 6),), [sm, st], {1: 0, 2: 1, 3: 2, 4: 3}, 6
    )(e1, r, lm, u, w)
    r, lm, u, w, es = call(
        kernel_inner, [VMEM] * 6, state + (f32(6, 6),), [sm, st], {1: 0, 2: 1, 3: 2, 4: 3, 5: 4}, 9
    )(a3, r, lm, u, w, es)
    sol, res, _, _, _, _ = call(
        kernel_last,
        [SMEM] + [VMEM] * 7,
        (whole, whole) + state,
        [sm, st],
        {4: 2, 5: 3, 6: 4, 7: 5},
        24,
        [fields, fields, dma(8)],
        (HBM, HBM) + (VMEM,) * 4,
    )(par, mod, b3, es, r, lm, u, w)
    return untiles(sol), untiles(res)


def solution(mesh):
    in_specs = (
        P("slab", None, "rve", None),
        P("slab", None, "rve", None),
        P("slab", "rve", None),
        P(),
    )
    out_specs = (P("slab", None, "rve", None), P("slab", None, "rve", None))
    return jax.shard_map(sweeps, mesh=mesh, in_specs=in_specs, out_specs=out_specs, check_vma=False)
```

```python
import jax
import jax.numpy as jnp
from jax import lax
from jax.experimental import pallas as pl
from jax.experimental.pallas import tpu as pltpu
from jax.sharding import PartitionSpec as P


OWN = 4
DEPTH = 6
INNER = 3
NODES = DEPTH + OWN + INNER
LAYERS = 16
N0 = DEPTH
L0 = 8

VMEM = pl.BlockSpec(memory_space=pltpu.VMEM)
SMEM = pl.BlockSpec(memory_space=pltpu.SMEM)
HBM = pl.BlockSpec(memory_space=pltpu.HBM)
ROW = (4, 8, 256)


def f32(*shape):
    return jax.ShapeDtypeStruct(shape + ROW, jnp.float32)


def even_rows():
    return lax.broadcasted_iota(jnp.int32, (8, 128), 0) % 2 == 0


def load_raw(ref, index, r):
    a = ref[index + (pl.ds(r, 8, stride=8), slice(None))]
    b = ref[index + (pl.ds(r + 4, 8, stride=8), slice(None))]
    even = even_rows()
    low = jnp.where(even, a, pltpu.roll(b, 1, 0))
    high = jnp.where(even, pltpu.roll(a, 7, 0), b)
    return jnp.concatenate([low, high], axis=1)


def store_raw(ref, index, r, value):
    low, high = value[:, :128], value[:, 128:]
    even = even_rows()
    ref[index + (pl.ds(r, 8, stride=8), slice(None))] = jnp.where(even, low, pltpu.roll(high, 1, 0))
    ref[index + (pl.ds(r + 4, 8, stride=8), slice(None))] = jnp.where(even, pltpu.roll(low, 7, 0), high)


def y_next(v):
    return pltpu.roll(v, 255, 1)


def y_prev(v):
    return pltpu.roll(v, 1, 1)


def x_prev(rows, r):
    return rows[r - 1] if r > 0 else pltpu.roll(rows[3], 1, 0)


def y_stage(sm, get, m):
    for c in range(3):
        for r in range(4):
            d = get(m, c, r)
            n = y_next(d)
            sm[m + L0, c, r] = d + n
            sm[m + L0, 3 + c, r] = n - d


def stress_step(sm, st, lm, m, get, save=None):
    first = prev = None

    def stress(z, nxt, r):
        x0, y1, z2, _, _, e, pd, qd = z
        gxx = nxt[0] - x0
        gyy = nxt[1] + y1
        gzz = nxt[2] + z2
        lame, mu = lm[m + L0, 0, r], lm[m + L0, 1, r]
        lt = lame * (gxx + gyy + gzz)
        mu2 = mu + mu
        values = (
            lt + mu2 * gxx,
            mu * (nxt[3] + pd),
            lt + mu2 * gyy,
            mu * (nxt[4] + qd),
            mu * (nxt[5] + e),
            lt + mu2 * gzz,
        )
        for i, v in enumerate(values):
            st[m + L0, i, r] = v
            if save is not None:
                save[i, r] = v

    for r in range(4):
        s, my, j = [], [], []
        for c in range(3):
            d = get(m + 1, c, r)
            n = y_next(d)
            su, mu_ = d + n, n - d
            sl, ml = sm[m + L0, c, r], sm[m + L0, 3 + c, r]
            sm[m + 1 + L0, c, r] = su
            sm[m + 1 + L0, 3 + c, r] = mu_
            s.append(sl + su)
            my.append(ml + mu_)
            j.append(su - sl)
        z = (s[0], my[1], j[2], my[0] + s[1], j[0] + s[2], j[1] + my[2], my[0] - s[1], j[0] - s[2])
        if r == 0:
            first = z
        else:
            stress(prev, z, r - 1)
        prev = z
    stress(prev, tuple(pltpu.roll(v, 7, 0) for v in first[:6]), 3)


def node_sums(st, m, r, above, below, top):
    upper = st.at[m + L0] if top is None else top
    new = [upper[i, r] if above else None for i in range(6)]
    old = [st[m - 1 + L0, i, r] if below else None for i in range(6)]

    def plus(i):
        return new[i] if not below else old[i] if not above else new[i] + old[i]

    def minus(i):
        return -new[i] if not below else old[i] if not above else old[i] - new[i]

    xx, xy, yy, xz, yz = (plus(i) for i in range(5))
    dxz, dyz, dzz = (minus(i) for i in range(3, 6))
    return (
        (xx + dxz, xy + dyz, xz + dzz),
        (dxz - xx, dyz - xy, dzz - xz),
        (xy, yy, yz),
    )


def node_step(st, m, finish, above=True, below=True, top=None):
    first = prev = None

    def out(pq, pp, ph, r):
        for c in range(3):
            g = pp[c] + pq[1][c]
            hh = ph[c] + pq[2][c]
            finish(m, c, r, (g - hh) + y_prev(g + hh))

    for r in range(4):
        pq = node_sums(st, m, r, above, below, top)
        if r == 0:
            first = pq
        else:
            out(pq, prev[0], prev[2], r)
        prev = pq
    roll = lambda v: pltpu.roll(v, 1, 0)
    out(first, tuple(map(roll, prev[0])), tuple(map(roll, prev[2])), 0)


def advance(refs, s, lo, hi, save=None, top=None, after=None):
    R, W, LM, U, sm, st = refs
    src, dst = s % 2, (s + 1) % 2

    def get(m, c, r):
        return W[m + N0, r] * R[src, m + N0, c, r]

    def finisher(own):
        def finish(m, c, r, k):
            old = R[src, m + N0, c, r]
            R[dst, m + N0, c, r] = old - k
            if own and after is None:
                U[m, c, r] = U[m, c, r] + W[m + N0, r] * old

        return finish

    def layer(m):
        if m < hi or (m == hi and top is None):
            stress_step(sm, st, LM, m, get)

    y_stage(sm, get, lo - 1)
    stress_step(sm, st, LM, lo - 1, get, save)
    layer(lo)
    for m in range(lo, hi + 1):
        layer(m + 1)
        node_step(st, m, finisher(0 <= m < OWN), top=top if m == hi else None)
        if after is not None:
            after(m)


def materials(LM, mod, load, m):
    for r in range(4):
        v = load(r)
        one, two = v == 1, v == 2
        for i in range(2):
            LM[m + L0, i, r] = jnp.where(two, mod[3 * i + 2], jnp.where(one, mod[3 * i + 1], mod[3 * i]))


def weights(W, LM, lo, hi):
    for m in range(lo, hi + 1):
        t = []
        for r in range(4):
            v = (LM[m - 1 + L0, 0, r] + LM[m + L0, 0, r]) + 4.0 * (LM[m - 1 + L0, 1, r] + LM[m + L0, 1, r])
            t.append(v)
        for r in range(4):
            v = t[r] + x_prev(t, r)
            W[m + N0, r] = 0.5 / (v + y_prev(v))


def sign_of(par):
    return (1 - 2 * par[0]).astype(jnp.float32)


def oriented(v, c, sign):
    return v * sign if c == 2 else v


def flipped(v, c):
    return -v if c == 2 else v


def kernel_own(par, mod_h, u_h, f_h, ph_h, R, LM, U, A1, B1, MOD, sm, st, W, u, f, ph, mod, sem):
    odd, sign = par[0], sign_of(par)
    copies = [
        pltpu.make_async_copy(src, dst, sem.at[i])
        for i, (src, dst) in enumerate(((mod_h, mod), (ph_h, ph), (u_h, u), (f_h, f)))
    ]
    for copy in copies:
        copy.start()
    plane = lambda m: jnp.where(odd == 1, 3 - m, m)
    copies[0].wait()
    for i in range(2):
        for j in range(3):
            MOD[3 * i + j] = jnp.full((8, 256), mod[i, j] * 0.0625, jnp.float32)
    copies[1].wait()
    for k in range(4):
        for r in range(4):
            v = load_raw(ph, (k,), r).astype(jnp.float32)
            A1[3 + k, r] = v
        materials(LM, MOD, lambda r: A1[3 + k, r], jnp.where(odd == 1, 2 - k, k))
    for j in range(3):
        B1[3 + j] = A1[3 + jnp.where(odd == 1, 3 - j, j)]
    weights(W, LM, 2, 2)
    copies[2].wait()
    for m in range(4):
        for c in range(3):
            for r in range(4):
                v = oriented(load_raw(u, (plane(m), c), r), c, sign)
                U[m, c, r] = v
                if m == 0:
                    B1[c, r] = v
                if m == 3:
                    A1[c, r] = v

    def get(m, c, r):
        return U[m, c, r]

    def finish(m, c, r, k):
        v = oriented(load_raw(f, (plane(m), c), r), c, sign) - k
        R[0, m + N0, c, r] = v
        if m < 3:
            B1[6 + 3 * m + c, r] = v if m < 2 else W[2 + N0, r] * v
        if m > 0:
            A1[7 + 3 * (3 - m) + c, r] = v

    y_stage(sm, get, 0)
    stress_step(sm, st, LM, 0, get)
    stress_step(sm, st, LM, 1, get)
    copies[3].wait()
    node_step(st, 0, finish, below=False)
    stress_step(sm, st, LM, 2, get)
    for m in range(1, 4):
        node_step(st, m, finish, above=m < 3)


def kernel_fin(par, mod, own, a1, r_in, lm_in, u_in, R, LM, U, P3, sm, st):
    odd = par[0]
    for k in range(4):
        materials(LM, mod, lambda r: a1[3 + k, r], jnp.where(odd == 1, 6 - k, 4 + k))
    P3[9] = own[3 + jnp.where(odd == 1, 0, 2)]
    for j in range(3):
        for r in range(4):
            v = a1[3 + jnp.where(odd == 1, 3 - j, max(j - 1, 0)), r]
            P3[10 + j, r] = jnp.where(odd == 1, v, own[6, r]) if j == 0 else v
    for c in range(3):
        v = flipped(a1[10 + c], c)
        R[0, 5 + N0, c] = v
        P3[6 + c] = v
        R[0, 6 + N0, c] = flipped(a1[13 + c], c)

    def get(m, c, r):
        return U[3, c, r] if m == 3 else flipped(a1[c, r], c)

    def finish(m, c, r, k):
        v = (R[0, 3 + N0, c, r] if m == 3 else flipped(a1[7 + c, r], c)) - k
        R[0, m + N0, c, r] = v
        P3[3 * (m - 3) + c, r] = v

    y_stage(sm, get, 3)
    stress_step(sm, st, LM, 3, get)
    node_step(st, 3, finish, below=False)
    node_step(st, 4, finish, above=False)


def kernel_near(r_in, lm_in, u_in, R, LM, U, W, EN, sm, st):
    weights(W, LM, 1, 6)
    refs = (R, W, LM, U, sm, st)
    advance(refs, 0, 2, 5, EN.at[0])
    advance(refs, 1, 3, 4, EN.at[1])


def kernel_mid(par, mod, b1, en, r_in, lm_in, u_in, w_in, R, LM, U, W, E1, PAY, edge, sm, st):
    odd = par[0]
    for j in range(3):
        materials(LM, mod, lambda r: b1[3 + j, r], jnp.where(odd == 1, -2 - j, -1 - j))
    weights(W, LM, -2, 0)
    W[-3 + N0] = jnp.ones(ROW, jnp.float32)

    def get(m, c, r):
        return flipped(b1[c, r], c) if m == -1 else U[0, c, r]

    def keep(m, c, r, k):
        edge[c, r] = k

    def take(m, c, r, k):
        R[0, N0, c, r] = R[0, N0, c, r] - k

    y_stage(sm, get, -1)
    stress_step(sm, st, LM, -1, get)
    node_step(st, -1, keep, below=False)
    node_step(st, 0, take, above=False)
    for j in range(3):
        for c in range(3):
            for r in range(4):
                v = flipped(b1[6 + 3 * j + c, r], c)
                R[0, -1 - j + N0, c, r] = v - edge[c, r] if j == 0 else v
    refs = (R, W, LM, U, sm, st)
    advance(refs, 0, -1, 1, E1.at[0], en.at[0])
    advance(refs, 1, 0, 2, E1.at[1], en.at[1])
    advance(refs, 2, 1, 3, E1.at[2])
    for j in range(3):
        for c in range(3):
            PAY[j, c] = R[1, 1 + j + N0, c]


def kernel_lead(e1, r_in, lm_in, u_in, w_in, R, LM, U, W, ES, sm, st):
    refs = (R, W, LM, U, sm, st)
    advance(refs, 0, -2, -2, ES.at[0], e1.at[0])
    advance(refs, 1, -1, -1, ES.at[1], e1.at[1])
    advance(refs, 2, 0, 0, ES.at[2], e1.at[2])
    advance(refs, 3, 1, 2, ES.at[3])


def kernel_inner(a3, r_in, lm_in, u_in, w_in, e_in, R, LM, U, W, ES, sm, st):
    for j in range(3):
        for c in range(3):
            R[1, 4 + j + N0, c] = flipped(a3[2 - j, c], c)
    refs = (R, W, LM, U, sm, st)
    advance(refs, 3, 3, 5)
    advance(refs, 4, 2, 4, ES.at[4])
    advance(refs, 5, 3, 3, ES.at[5])


def kernel_last(par, mod, b3, es, r_in, lm_in, u_in, w_in, sol_h, res_h, R, LM, U, W, sm, st, sol, res, sem):
    odd, sign = par[0], sign_of(par)
    started = []

    def put(buf, dst, i, m, get):
        for c in range(3):
            for r in range(4):
                store_raw(buf, (m, c), r, oriented(get(c, r), c, sign))
        copy = pltpu.make_async_copy(buf.at[m], dst.at[jnp.where(odd == 1, 3 - m, m)], sem.at[2 * m + i])
        copy.start()
        started.append(copy)

    def put_res(m):
        put(res, res_h, 1, m, lambda c, r: R[0, m + N0, c, r])

    put(sol, sol_h, 0, 3, lambda c, r: U[3, c, r])
    put_res(3)
    for j in range(4):
        materials(LM, mod, lambda r: b3[9 + j, r], -4 - j)
    weights(W, LM, -6, -3)
    for c in range(3):
        R[0, -3 + N0, c] = R[0, -3 + N0, c] / W[-3 + N0]
        for j in range(3):
            R[0, -4 - j + N0, c] = flipped(b3[3 * j + c], c)
    refs = (R, W, LM, U, sm, st)
    for s in range(5):
        advance(refs, s, s - 5, s - 3, top=es.at[s])
    for m in range(3):
        put(sol, sol_h, 0, m, lambda c, r: U[m, c, r] + W[m + N0, r] * R[1, m + N0, c, r])
    advance(refs, 5, 0, 2, top=es.at[5], after=put_res)
    for copy in started:
        copy.wait()


def call(kernel, in_specs, out_shape, scratch, alias, planes, extra=(), out_specs=None):
    return pl.pallas_call(
        kernel,
        out_shape=out_shape,
        in_specs=in_specs,
        out_specs=out_specs or tuple(VMEM for _ in out_shape),
        scratch_shapes=[pltpu.VMEM(s + ROW, jnp.float32) for s in scratch] + list(extra),
        input_output_aliases=alias,
        compiler_params=pltpu.CompilerParams(vmem_limit_bytes=14 << 20),
        cost_estimate=pl.CostEstimate(flops=planes * 700000, bytes_accessed=planes * 500000, transcendentals=0),
    )


def tiles(x):
    lead = x.shape[:-2]
    return x.reshape(lead + (4, 8, 2, 128)).swapaxes(-3, -2).reshape(lead + (64, 128))


def untiles(x):
    lead = x.shape[:-2]
    return x.reshape(lead + (4, 2, 8, 128)).swapaxes(-3, -2).reshape(lead + (32, 256))


def sweeps(displacement, load, phase, moduli):
    count = lax.axis_size("slab")
    odd = lax.bitwise_and(lax.axis_index("slab"), 1)
    par = odd.reshape(1).astype(jnp.int32)
    inside = [(i, i ^ 1) for i in range(count)]
    across = [(i, (i - 1) % count if i % 2 == 0 else (i + 1) % count) for i in range(count)]

    def send(v, pairs):
        return lax.ppermute(v, "slab", pairs)

    sm, st = (LAYERS, 6), (LAYERS, 6)
    R, LM, U, W = f32(2, NODES, 3), f32(LAYERS, 2), f32(OWN, 3), f32(NODES)
    state = (R, LM, U, W)
    dma = lambda n: pltpu.SemaphoreType.DMA((n,))
    block = lambda n, kind=jnp.float32: pltpu.VMEM((n, 64, 128), kind)
    in_hbm = lambda v: pltpu.with_memory_space_constraint(v, pltpu.HBM)
    u_t, f_t, ph_t = (in_hbm(tiles(v)) for v in (displacement, load, phase))
    moduli = in_hbm(moduli)

    whole = jax.ShapeDtypeStruct((OWN, 3, 64, 128), jnp.float32)
    six = jax.ShapeDtypeStruct((6, 8, 256), jnp.float32)
    fields = pltpu.VMEM((OWN, 3, 64, 128), jnp.float32)
    r, lm, u, pay, pay1, mod = call(
        kernel_own,
        [SMEM] + [HBM] * 4,
        (R, LM, U, f32(16), f32(15), six),
        [sm, st, (NODES,)],
        {},
        4,
        [fields, fields, block(4, jnp.int32), pltpu.SMEM((2, 3), jnp.float32), dma(4)],
    )(par, moduli, u_t, f_t, ph_t)
    b1 = send(pay1, across)
    a1 = send(pay, inside)
    r, lm, u, pay3 = call(
        kernel_fin, [SMEM] + [VMEM] * 6, (R, LM, U, f32(13)), [sm, st], {4: 0, 5: 1, 6: 2}, 2
    )(par, mod, pay, a1, r, lm, u)
    b3 = send(pay3, across)
    r, lm, u, w, en = call(
        kernel_near, [VMEM] * 3, state + (f32(2, 6),), [sm, st], {0: 0, 1: 1, 2: 2}, 8
    )(r, lm, u)
    r, lm, u, w, e1, pay = call(
        kernel_mid,
        [SMEM] + [VMEM] * 7,
        state + (f32(3, 6), f32(3, 3)),
        [(3,), sm, st],
        {4: 0, 5: 1, 6: 2, 7: 3},
        14,
    )(par, mod, b1, en, r, lm, u, w)
    a3 = send(pay, inside)
    r, lm, u, w, es = call(
        kernel_lead, [VMEM] * 5, state + (f32(6, 6),), [sm, st], {1: 0, 2: 1, 3: 2, 4: 3}, 6
    )(e1, r, lm, u, w)
    r, lm, u, w, es = call(
        kernel_inner, [VMEM] * 6, state + (f32(6, 6),), [sm, st], {1: 0, 2: 1, 3: 2, 4: 3, 5: 4}, 9
    )(a3, r, lm, u, w, es)
    sol, res, _, _, _, _ = call(
        kernel_last,
        [SMEM] + [VMEM] * 7,
        (whole, whole) + state,
        [sm, st],
        {4: 2, 5: 3, 6: 4, 7: 5},
        24,
        [fields, fields, dma(8)],
        (HBM, HBM) + (VMEM,) * 4,
    )(par, mod, b3, es, r, lm, u, w)
    return untiles(sol), untiles(res)


def solution(mesh):
    in_specs = (
        P("slab", None, "rve", None),
        P("slab", None, "rve", None),
        P("slab", "rve", None),
        P(),
    )
    out_specs = (P("slab", None, "rve", None), P("slab", None, "rve", None))
    return jax.shard_map(sweeps, mesh=mesh, in_specs=in_specs, out_specs=out_specs, check_vma=False)
```

```python
import jax
import jax.numpy as jnp
from jax import lax
from jax.experimental import pallas as pl
from jax.experimental.pallas import tpu as pltpu
from jax.sharding import PartitionSpec as P


OWN = 4
DEPTH = 6
INNER = 3
NODES = DEPTH + OWN + INNER
LAYERS = 16
N0 = DEPTH
L0 = 8

VMEM = pl.BlockSpec(memory_space=pltpu.VMEM)
SMEM = pl.BlockSpec(memory_space=pltpu.SMEM)
HBM = pl.BlockSpec(memory_space=pltpu.HBM)
ROW = (4, 8, 256)


def f32(*shape):
    return jax.ShapeDtypeStruct(shape + ROW, jnp.float32)


def even_rows():
    return lax.broadcasted_iota(jnp.int32, (8, 128), 0) % 2 == 0


def load_raw(ref, index, r):
    a = ref[index + (pl.ds(r, 8, stride=8), slice(None))]
    b = ref[index + (pl.ds(r + 4, 8, stride=8), slice(None))]
    even = even_rows()
    low = jnp.where(even, a, pltpu.roll(b, 1, 0))
    high = jnp.where(even, pltpu.roll(a, 7, 0), b)
    return jnp.concatenate([low, high], axis=1)


def store_raw(ref, index, r, value):
    low, high = value[:, :128], value[:, 128:]
    even = even_rows()
    ref[index + (pl.ds(r, 8, stride=8), slice(None))] = jnp.where(even, low, pltpu.roll(high, 1, 0))
    ref[index + (pl.ds(r + 4, 8, stride=8), slice(None))] = jnp.where(even, pltpu.roll(low, 7, 0), high)


def y_next(v):
    return pltpu.roll(v, 255, 1)


def y_prev(v):
    return pltpu.roll(v, 1, 1)


def x_prev(rows, r):
    return rows[r - 1] if r > 0 else pltpu.roll(rows[3], 1, 0)


def y_stage(sm, get, m):
    for c in range(3):
        for r in range(4):
            d = get(m, c, r)
            n = y_next(d)
            sm[m + L0, c, r] = d + n
            sm[m + L0, 3 + c, r] = n - d


def stress_step(sm, st, lm, m, get, save=None):
    first = prev = None

    def stress(z, nxt, r):
        x0, y1, z2, _, _, e, pd, qd = z
        gxx = nxt[0] - x0
        gyy = nxt[1] + y1
        gzz = nxt[2] + z2
        lame, mu = lm[m + L0, 0, r], lm[m + L0, 1, r]
        lt = lame * (gxx + gyy + gzz)
        mu2 = mu + mu
        values = (
            lt + mu2 * gxx,
            mu * (nxt[3] + pd),
            lt + mu2 * gyy,
            mu * (nxt[4] + qd),
            mu * (nxt[5] + e),
            lt + mu2 * gzz,
        )
        for i, v in enumerate(values):
            st[m + L0, i, r] = v
            if save is not None:
                save[i, r] = v

    for r in range(4):
        s, my, j = [], [], []
        for c in range(3):
            d = get(m + 1, c, r)
            n = y_next(d)
            su, mu_ = d + n, n - d
            sl, ml = sm[m + L0, c, r], sm[m + L0, 3 + c, r]
            sm[m + 1 + L0, c, r] = su
            sm[m + 1 + L0, 3 + c, r] = mu_
            s.append(sl + su)
            my.append(ml + mu_)
            j.append(su - sl)
        z = (s[0], my[1], j[2], my[0] + s[1], j[0] + s[2], j[1] + my[2], my[0] - s[1], j[0] - s[2])
        if r == 0:
            first = z
        else:
            stress(prev, z, r - 1)
        prev = z
    stress(prev, tuple(pltpu.roll(v, 7, 0) for v in first[:6]), 3)


def node_sums(st, m, r, above, below, top, base):
    upper = st.at[m + L0] if top is None else top
    new = [upper[i, r] if above else None for i in range(6)]
    lower = st.at[m - 1 + L0] if base is None else base
    old = [lower[i, r] if below else None for i in range(6)]

    def plus(i):
        return new[i] if not below else old[i] if not above else new[i] + old[i]

    def minus(i):
        return -new[i] if not below else old[i] if not above else old[i] - new[i]

    xx, xy, yy, xz, yz = (plus(i) for i in range(5))
    dxz, dyz, dzz = (minus(i) for i in range(3, 6))
    return (
        (xx + dxz, xy + dyz, xz + dzz),
        (dxz - xx, dyz - xy, dzz - xz),
        (xy, yy, yz),
    )


def node_step(st, m, finish, above=True, below=True, top=None, base=None):
    first = prev = None

    def out(pq, pp, ph, r):
        for c in range(3):
            g = pp[c] + pq[1][c]
            hh = ph[c] + pq[2][c]
            finish(m, c, r, (g - hh) + y_prev(g + hh))

    for r in range(4):
        pq = node_sums(st, m, r, above, below, top, base)
        if r == 0:
            first = pq
        else:
            out(pq, prev[0], prev[2], r)
        prev = pq
    roll = lambda v: pltpu.roll(v, 1, 0)
    out(first, tuple(map(roll, prev[0])), tuple(map(roll, prev[2])), 0)


def advance(refs, s, lo, hi, save=None, top=None, after=None, base=None, keep=None):
    R, W, LM, U, sm, st = refs
    src, dst = s % 2, (s + 1) % 2

    def get(m, c, r):
        return W[m + N0, r] * R[src, m + N0, c, r]

    def finisher(own):
        def finish(m, c, r, k):
            old = R[src, m + N0, c, r]
            R[dst, m + N0, c, r] = old - k
            if own and after is None:
                U[m, c, r] = U[m, c, r] + W[m + N0, r] * old

        return finish

    def layer(m):
        if m < hi or (m == hi and top is None):
            stress_step(sm, st, LM, m, get, keep if m == hi else None)

    if base is None:
        y_stage(sm, get, lo - 1)
        stress_step(sm, st, LM, lo - 1, get, save)
    else:
        y_stage(sm, get, lo)
    layer(lo)
    for m in range(lo, hi + 1):
        layer(m + 1)
        node_step(st, m, finisher(0 <= m < OWN), top=top if m == hi else None, base=base if m == lo else None)
        if after is not None:
            after(m)


def materials(LM, mod, load, m):
    for r in range(4):
        v = load(r)
        one, two = v == 1, v == 2
        for i in range(2):
            LM[m + L0, i, r] = jnp.where(two, mod[3 * i + 2], jnp.where(one, mod[3 * i + 1], mod[3 * i]))


def weights(W, LM, lo, hi):
    for m in range(lo, hi + 1):
        t = []
        for r in range(4):
            v = (LM[m - 1 + L0, 0, r] + LM[m + L0, 0, r]) + 4.0 * (LM[m - 1 + L0, 1, r] + LM[m + L0, 1, r])
            t.append(v)
        for r in range(4):
            v = t[r] + x_prev(t, r)
            W[m + N0, r] = 0.5 / (v + y_prev(v))


def sign_of(par):
    return (1 - 2 * par[0]).astype(jnp.float32)


def oriented(v, c, sign):
    return v * sign if c == 2 else v


def flipped(v, c):
    return -v if c == 2 else v


def kernel_own(par, mod_h, u_h, f_h, ph_h, R, LM, U, A1, B1, MOD, sm, st, W, u, f, ph, mod, sem):
    odd, sign = par[0], sign_of(par)
    copies = [
        pltpu.make_async_copy(src, dst, sem.at[i])
        for i, (src, dst) in enumerate(((mod_h, mod), (ph_h, ph), (u_h, u), (f_h, f)))
    ]
    for copy in copies:
        copy.start()
    plane = lambda m: jnp.where(odd == 1, 3 - m, m)
    copies[0].wait()
    for i in range(2):
        for j in range(3):
            MOD[3 * i + j] = jnp.full((8, 256), mod[i, j] * 0.0625, jnp.float32)
    copies[1].wait()
    for k in range(4):
        for r in range(4):
            v = load_raw(ph, (k,), r).astype(jnp.float32)
            A1[3 + k, r] = v
        materials(LM, MOD, lambda r: A1[3 + k, r], jnp.where(odd == 1, 2 - k, k))
    for j in range(3):
        B1[3 + j] = A1[3 + jnp.where(odd == 1, 3 - j, j)]
    weights(W, LM, 2, 2)
    copies[2].wait()
    for m in range(4):
        for c in range(3):
            for r in range(4):
                v = oriented(load_raw(u, (plane(m), c), r), c, sign)
                U[m, c, r] = v
                if m == 0:
                    B1[c, r] = v
                if m == 3:
                    A1[c, r] = v

    def get(m, c, r):
        return U[m, c, r]

    def finish(m, c, r, k):
        v = oriented(load_raw(f, (plane(m), c), r), c, sign) - k
        R[0, m + N0, c, r] = v
        if m < 3:
            B1[6 + 3 * m + c, r] = v if m < 2 else W[2 + N0, r] * v
        if m > 0:
            A1[7 + 3 * (3 - m) + c, r] = v

    y_stage(sm, get, 0)
    stress_step(sm, st, LM, 0, get)
    stress_step(sm, st, LM, 1, get)
    copies[3].wait()
    node_step(st, 0, finish, below=False)
    stress_step(sm, st, LM, 2, get)
    for m in range(1, 4):
        node_step(st, m, finish, above=m < 3)


def kernel_fin(par, mod, own, a1, r_in, lm_in, u_in, R, LM, U, P3, sm, st):
    odd = par[0]
    for k in range(4):
        materials(LM, mod, lambda r: a1[3 + k, r], jnp.where(odd == 1, 6 - k, 4 + k))
    P3[9] = own[3 + jnp.where(odd == 1, 0, 2)]
    for j in range(3):
        for r in range(4):
            v = a1[3 + jnp.where(odd == 1, 3 - j, max(j - 1, 0)), r]
            P3[10 + j, r] = jnp.where(odd == 1, v, own[6, r]) if j == 0 else v
    for c in range(3):
        v = flipped(a1[10 + c], c)
        R[0, 5 + N0, c] = v
        P3[6 + c] = v
        R[0, 6 + N0, c] = flipped(a1[13 + c], c)

    def get(m, c, r):
        return U[3, c, r] if m == 3 else flipped(a1[c, r], c)

    def finish(m, c, r, k):
        v = (R[0, 3 + N0, c, r] if m == 3 else flipped(a1[7 + c, r], c)) - k
        R[0, m + N0, c, r] = v
        P3[3 * (m - 3) + c, r] = v

    y_stage(sm, get, 3)
    stress_step(sm, st, LM, 3, get)
    node_step(st, 3, finish, below=False)
    node_step(st, 4, finish, above=False)


def kernel_near(r_in, lm_in, u_in, R, LM, U, W, EN, sm, st):
    weights(W, LM, 1, 6)
    refs = (R, W, LM, U, sm, st)
    advance(refs, 0, 2, 5, EN.at[0])
    advance(refs, 1, 3, 4, EN.at[1])


def kernel_mid(par, mod, b1, en, r_in, lm_in, u_in, w_in, R, LM, U, W, E1, PAY, edge, sm, st):
    odd = par[0]
    for j in range(3):
        materials(LM, mod, lambda r: b1[3 + j, r], jnp.where(odd == 1, -2 - j, -1 - j))
    weights(W, LM, -2, 0)
    W[-3 + N0] = jnp.ones(ROW, jnp.float32)

    def get(m, c, r):
        return flipped(b1[c, r], c) if m == -1 else U[0, c, r]

    def keep(m, c, r, k):
        edge[c, r] = k

    def take(m, c, r, k):
        R[0, N0, c, r] = R[0, N0, c, r] - k

    y_stage(sm, get, -1)
    stress_step(sm, st, LM, -1, get)
    node_step(st, -1, keep, below=False)
    node_step(st, 0, take, above=False)
    for j in range(3):
        for c in range(3):
            for r in range(4):
                v = flipped(b1[6 + 3 * j + c, r], c)
                R[0, -1 - j + N0, c, r] = v - edge[c, r] if j == 0 else v
    refs = (R, W, LM, U, sm, st)
    advance(refs, 0, -1, 1, E1.at[0], en.at[0])
    advance(refs, 1, 0, 2, E1.at[1], en.at[1])
    advance(refs, 2, 1, 3, E1.at[2])
    for j in range(3):
        for c in range(3):
            PAY[j, c] = R[1, 1 + j + N0, c]


def kernel_lead(e1, r_in, lm_in, u_in, w_in, R, LM, U, W, ES, sm, st):
    refs = (R, W, LM, U, sm, st)
    advance(refs, 0, -2, -2, ES.at[0], e1.at[0])
    advance(refs, 1, -1, -1, ES.at[1], e1.at[1])
    advance(refs, 2, 0, 0, ES.at[2], e1.at[2])
    advance(refs, 3, 1, 2, ES.at[3], keep=ES.at[5])


def kernel_inner(a3, r_in, lm_in, u_in, w_in, e_in, R, LM, U, W, ES, sm, st):
    for j in range(3):
        for c in range(3):
            R[1, 4 + j + N0, c] = flipped(a3[2 - j, c], c)
    refs = (R, W, LM, U, sm, st)
    advance(refs, 3, 3, 5, base=ES.at[5])
    advance(refs, 4, 2, 4, ES.at[4])
    advance(refs, 5, 3, 3, ES.at[5])


def kernel_last(par, mod, b3, es, r_in, lm_in, u_in, w_in, sol_h, res_h, R, LM, U, W, sm, st, sol, res, sem):
    odd, sign = par[0], sign_of(par)
    started = []

    def put(buf, dst, i, m, get):
        for c in range(3):
            for r in range(4):
                store_raw(buf, (m, c), r, oriented(get(c, r), c, sign))
        copy = pltpu.make_async_copy(buf.at[m], dst.at[jnp.where(odd == 1, 3 - m, m)], sem.at[2 * m + i])
        copy.start()
        started.append(copy)

    def put_res(m):
        put(res, res_h, 1, m, lambda c, r: R[0, m + N0, c, r])

    put(sol, sol_h, 0, 3, lambda c, r: U[3, c, r])
    put_res(3)
    for j in range(4):
        materials(LM, mod, lambda r: b3[9 + j, r], -4 - j)
    weights(W, LM, -6, -3)
    for c in range(3):
        R[0, -3 + N0, c] = R[0, -3 + N0, c] / W[-3 + N0]
        for j in range(3):
            R[0, -4 - j + N0, c] = flipped(b3[3 * j + c], c)
    refs = (R, W, LM, U, sm, st)
    for s in range(5):
        advance(refs, s, s - 5, s - 3, top=es.at[s])
    for m in range(3):
        put(sol, sol_h, 0, m, lambda c, r: U[m, c, r] + W[m + N0, r] * R[1, m + N0, c, r])
    advance(refs, 5, 0, 2, top=es.at[5], after=put_res)
    for copy in started:
        copy.wait()


def call(kernel, in_specs, out_shape, scratch, alias, planes, extra=(), out_specs=None):
    return pl.pallas_call(
        kernel,
        out_shape=out_shape,
        in_specs=in_specs,
        out_specs=out_specs or tuple(VMEM for _ in out_shape),
        scratch_shapes=[pltpu.VMEM(s + ROW, jnp.float32) for s in scratch] + list(extra),
        input_output_aliases=alias,
        compiler_params=pltpu.CompilerParams(vmem_limit_bytes=14 << 20),
        cost_estimate=pl.CostEstimate(flops=planes * 700000, bytes_accessed=planes * 500000, transcendentals=0),
    )


def tiles(x):
    lead = x.shape[:-2]
    return x.reshape(lead + (4, 8, 2, 128)).swapaxes(-3, -2).reshape(lead + (64, 128))


def untiles(x):
    lead = x.shape[:-2]
    return x.reshape(lead + (4, 2, 8, 128)).swapaxes(-3, -2).reshape(lead + (32, 256))


def sweeps(displacement, load, phase, moduli):
    count = lax.axis_size("slab")
    odd = lax.bitwise_and(lax.axis_index("slab"), 1)
    par = odd.reshape(1).astype(jnp.int32)
    inside = [(i, i ^ 1) for i in range(count)]
    across = [(i, (i - 1) % count if i % 2 == 0 else (i + 1) % count) for i in range(count)]

    def send(v, pairs):
        return lax.ppermute(v, "slab", pairs)

    sm, st = (LAYERS, 6), (LAYERS, 6)
    R, LM, U, W = f32(2, NODES, 3), f32(LAYERS, 2), f32(OWN, 3), f32(NODES)
    state = (R, LM, U, W)
    dma = lambda n: pltpu.SemaphoreType.DMA((n,))
    block = lambda n, kind=jnp.float32: pltpu.VMEM((n, 64, 128), kind)
    in_hbm = lambda v: pltpu.with_memory_space_constraint(v, pltpu.HBM)
    u_t, f_t, ph_t = (in_hbm(tiles(v)) for v in (displacement, load, phase))
    moduli = in_hbm(moduli)

    whole = jax.ShapeDtypeStruct((OWN, 3, 64, 128), jnp.float32)
    six = jax.ShapeDtypeStruct((6, 8, 256), jnp.float32)
    fields = pltpu.VMEM((OWN, 3, 64, 128), jnp.float32)
    r, lm, u, pay, pay1, mod = call(
        kernel_own,
        [SMEM] + [HBM] * 4,
        (R, LM, U, f32(16), f32(15), six),
        [sm, st, (NODES,)],
        {},
        4,
        [fields, fields, block(4, jnp.int32), pltpu.SMEM((2, 3), jnp.float32), dma(4)],
    )(par, moduli, u_t, f_t, ph_t)
    b1 = send(pay1, across)
    a1 = send(pay, inside)
    r, lm, u, pay3 = call(
        kernel_fin, [SMEM] + [VMEM] * 6, (R, LM, U, f32(13)), [sm, st], {4: 0, 5: 1, 6: 2}, 2
    )(par, mod, pay, a1, r, lm, u)
    b3 = send(pay3, across)
    r, lm, u, w, en = call(
        kernel_near, [VMEM] * 3, state + (f32(2, 6),), [sm, st], {0: 0, 1: 1, 2: 2}, 8
    )(r, lm, u)
    r, lm, u, w, e1, pay = call(
        kernel_mid,
        [SMEM] + [VMEM] * 7,
        state + (f32(3, 6), f32(3, 3)),
        [(3,), sm, st],
        {4: 0, 5: 1, 6: 2, 7: 3},
        14,
    )(par, mod, b1, en, r, lm, u, w)
    a3 = send(pay, inside)
    r, lm, u, w, es = call(
        kernel_lead, [VMEM] * 5, state + (f32(6, 6),), [sm, st], {1: 0, 2: 1, 3: 2, 4: 3}, 6
    )(e1, r, lm, u, w)
    r, lm, u, w, es = call(
        kernel_inner, [VMEM] * 6, state + (f32(6, 6),), [sm, st], {1: 0, 2: 1, 3: 2, 4: 3, 5: 4}, 9
    )(a3, r, lm, u, w, es)
    sol, res, _, _, _, _ = call(
        kernel_last,
        [SMEM] + [VMEM] * 7,
        (whole, whole) + state,
        [sm, st],
        {4: 2, 5: 3, 6: 4, 7: 5},
        24,
        [fields, fields, dma(8)],
        (HBM, HBM) + (VMEM,) * 4,
    )(par, mod, b3, es, r, lm, u, w)
    return untiles(sol), untiles(res)


def solution(mesh):
    in_specs = (
        P("slab", None, "rve", None),
        P("slab", None, "rve", None),
        P("slab", "rve", None),
        P(),
    )
    out_specs = (P("slab", None, "rve", None), P("slab", None, "rve", None))
    return jax.shard_map(sweeps, mesh=mesh, in_specs=in_specs, out_specs=out_specs, check_vma=False)
```
